32 devices in a mesh: groups: 2 (over y), wide: 8 (over z, x), narrow: 2 (over core).
Axes of the slice: x: 2, y: 2, z: 4, core: 2. Of those that a mesh axis runs over, the one named last changes fastest.
Arguments:
- pieces: bfloat16 [2, 1024, 8192], P(None, ('groups', 'wide'), 'narrow'), parts along dimension 1, may hold values from -6 to 6
- destination: int32 [512], P('wide'), may hold values from 0 to 511, as said below
- first_offset: int32 [512], P('wide'), may hold values from 0 to 6144, as said below
- valid_length: int32 [512], P('wide'), may hold values from 2048 to 8192
- midpoint_factor: float32 [1024, 128], P(('groups', 'wide')), parts along dimension 0, may hold values from -0.3 to 0.3
- offset_factor: float32 [16384, 128], P(('groups', 'narrow')), parts along dimension 0, may hold values from -6 to 6
- threshold: float32 [16384], P(('groups', 'narrow')), parts along dimension 0, may hold values from 0.3 to 3
Outputs:
- sparse: bfloat16 [2, 1024, 8192], P(None, ('groups', 'wide'), 'narrow'), parts along dimension 1
- new_midpoint: float32 [1024, 128], P(('groups', 'wide')), parts along dimension 0
- new_offset: float32 [16384, 128], P(('groups', 'narrow')), parts along dimension 0
The draws below stay inside these ranges and needn't reach their ends.
There are 2 independent parts, one for each index of `groups`. The reference program is written for one: setup_inputs(seed, part) draws one part's arguments, and reference() takes and returns one part's arrays. A program takes and returns all parts, laid end to end along the dimension named above; an argument that names none is the same for every part. Nothing has to cross between parts.
Inputs may be any that keep to these rules, and one draw needn't show every extreme that they name: destination is a permutation of the midpoint rows; the 64 segments of one device (aligned blocks) name at most 16 rows of any aligned block of 64 midpoint rows, and exactly 16 rows of some block. first_offset + valid_length <= 8192.
All inputs are finite; a program needn't handle non-finite values.
Results may differ from the reference program's by a relative error of at most 0.005.
Values may be sent and summed in bfloat16 or wider, within the bound.
No kernel may reach another device: no remote copies, remote signals or barrier semaphores. Data moves between devices by JAX's collectives and lax.ppermute only.
A program may use at most 64 MiB of HBM per device.

```python
import math
from functools import partial
import jax
import jax.numpy as jnp
from jax import lax

OFF = 8192
RANK = 64
ROWS_DEV = 64
ITERS = 2
MIDS = 512


def shuffled(count, subkey):
    return jax.random.permutation(subkey, count).astype(jnp.int32)


def route_table(key):
    block_count = MIDS // ROWS_DEV
    average = ROWS_DEV // block_count
    keys = jax.random.split(jax.random.fold_in(key, 11), 3)
    order = jax.random.permutation(keys[0], block_count).astype(jnp.int32)
    follow = jnp.roll(order, -1)
    column = jnp.arange(block_count, dtype=jnp.int32)
    counts = average + average * (column[None, :] == order[:, None]).astype(jnp.int32) - average * (column[None, :] == follow[:, None]).astype(jnp.int32)
    cumulative = jnp.cumsum(counts, axis=1)
    src_begin = cumulative - counts
    dst_begin = jnp.cumsum(counts, axis=0) - counts
    position = jnp.arange(ROWS_DEV, dtype=jnp.int32)
    target = jnp.sum((cumulative[:, None, :] <= position[None, :, None]).astype(jnp.int32), axis=2)
    within = position[None, :] - jnp.take_along_axis(src_begin, target, 1)
    arrival = jnp.take_along_axis(dst_begin, target, 1) + within
    local_orders = jax.vmap(partial(shuffled, ROWS_DEV))(jax.random.split(keys[1], block_count))
    landing = local_orders[target, arrival]
    value = target * ROWS_DEV + landing
    senders = jax.vmap(partial(shuffled, ROWS_DEV))(jax.random.split(keys[2], block_count))
    table = jnp.zeros((block_count, ROWS_DEV), jnp.int32)
    table = table.at[column[:, None], senders].set(value)
    return table.reshape(MIDS)


def segment_table(key):
    keys = jax.random.split(jax.random.fold_in(key, 23), 2)
    valid = jax.random.randint(keys[0], (MIDS,), OFF // 4, OFF + 1, dtype=jnp.int32)
    begin = jax.random.randint(keys[1], (MIDS,), 0, OFF + 1, dtype=jnp.int32) % (OFF - valid + 1)
    return (begin, valid)


def draw_destination(key, part):
    return route_table(key)


def draw_first_offset(key, part):
    return segment_table(key)[0]


def draw_valid_length(key, part):
    return segment_table(key)[1]


def block_levels(key, shape, shards, least, largest):
    def one(dim, parts):
        steps = jax.random.uniform(jax.random.fold_in(jax.random.fold_in(key, 6), dim), (parts,), jnp.float32, least / len(shards), largest / len(shards))
        return jnp.repeat(jnp.exp(steps), shape[dim] // parts).reshape((-1,) + (1,) * (len(shape) - dim - 1))

    level = one(*shards[0])
    for cut in shards[1:]:
        level = level * one(*cut)
    return level


def bell_draw(own_key, dims, spread, limit, shards=(), kind=jnp.bfloat16):
    loudness = block_levels(own_key, dims, shards, -0.22, 0.18) if shards else 1.0
    array = jax.random.normal(own_key, dims, jnp.float32) * spread * loudness
    return jnp.minimum(jnp.maximum(array, -limit), limit).astype(kind)


def setup_inputs(seed: int = 0, part: int = 0) -> dict:
    streams_of = jax.random.split(jax.random.key(seed), 8)
    part_keys = jax.random.split(jax.random.fold_in(streams_of[7], part), 8)
    return {
        "pieces": bell_draw(part_keys[0], (2, MIDS, OFF), 1.0, 6.0, ((1, 8), (2, 2))),
        "destination": draw_destination(jax.random.fold_in(streams_of[7], 71), part),
        "first_offset": draw_first_offset(jax.random.fold_in(streams_of[7], 71), part),
        "valid_length": draw_valid_length(jax.random.fold_in(streams_of[7], 71), part),
        "midpoint_factor": bell_draw(part_keys[4], (MIDS, 2 * RANK), 0.05, 0.3, ((0, 8),), jnp.float32),
        "offset_factor": bell_draw(part_keys[5], (OFF, 2 * RANK), 1.0, 6.0, ((0, 2),), jnp.float32),
        "threshold": jnp.clip(jnp.exp(math.log(3.0) - 2.3025851 * jax.random.uniform(part_keys[6], (OFF,), jnp.float32) ** block_levels(part_keys[6], (OFF,), ((0, 2),), -0.2, 0.2)), 0.3, 3.0),
    }


epsilon = 1e-06

def reference(pieces, destination, first_offset, valid_length, midpoint_factor, offset_factor, threshold):
    total_rows = pieces.shape[1]
    col_total = pieces.shape[2]
    half_rank = midpoint_factor.shape[1] // 2
    block_total = total_rows // ROWS_DEV
    columns = jnp.arange(col_total, dtype=jnp.int32)
    left_factor = midpoint_factor
    right_factor = offset_factor
    sparse_blocks = None
    for sweep in range(ITERS):
        right_low = right_factor.astype(jnp.bfloat16)
        right_turn = jnp.concatenate([-right_factor[:, half_rank:], right_factor[:, :half_rank]], 1).astype(jnp.bfloat16)
        left_seg = left_factor.astype(jnp.bfloat16)[destination]
        left_turn = jnp.concatenate([left_seg[:, half_rank:], -left_seg[:, :half_rank]], 1)
        right_norm = lax.optimization_barrier(jnp.sum(right_factor[:, :half_rank] ** 2 + right_factor[:, half_rank:] ** 2, 0))
        left_norm = lax.optimization_barrier(jnp.sum(left_factor[:, :half_rank] ** 2 + left_factor[:, half_rank:] ** 2, 0))

        def one_block(offset_grad, block_index):
            first_row = block_index * ROWS_DEV
            observed = lax.dynamic_slice_in_dim(pieces, first_row, ROWS_DEV, 1).astype(jnp.float32)
            begin_col = lax.dynamic_slice_in_dim(first_offset, first_row, ROWS_DEV, 0)
            span_cols = lax.dynamic_slice_in_dim(valid_length, first_row, ROWS_DEV, 0)
            inside = (columns[None, :] >= begin_col[:, None]) & (columns[None, :] < (begin_col + span_cols)[:, None])
            row_factor = lax.dynamic_slice_in_dim(left_seg, first_row, ROWS_DEV, 0)
            row_turn = lax.dynamic_slice_in_dim(left_turn, first_row, ROWS_DEV, 0)
            model_real = jnp.dot(row_factor, right_low.T, preferred_element_type=jnp.float32)
            model_imag = jnp.dot(row_factor, right_turn.T, preferred_element_type=jnp.float32)
            resid_real = jnp.where(inside, observed[0] - model_real, jnp.float32(0.0))
            resid_imag = jnp.where(inside, observed[1] - model_imag, jnp.float32(0.0))
            magnitude = jnp.sqrt(resid_real * resid_real + resid_imag * resid_imag)
            factor = jnp.maximum(magnitude - threshold[None, :], 0.0) / jnp.maximum(magnitude, threshold[None, :])
            sparse_real = resid_real * factor
            sparse_imag = resid_imag * factor
            error_real = (resid_real - sparse_real).astype(jnp.bfloat16)
            error_imag = (resid_imag - sparse_imag).astype(jnp.bfloat16)
            row_grad = jnp.dot(error_real, right_low, preferred_element_type=jnp.float32) + jnp.dot(error_imag, right_turn, preferred_element_type=jnp.float32)
            offset_grad = offset_grad + jnp.dot(error_real.T, row_factor, preferred_element_type=jnp.float32) + jnp.dot(error_imag.T, row_turn, preferred_element_type=jnp.float32)
            return (offset_grad, (jnp.stack([sparse_real, sparse_imag]), row_grad))
        start_grad = jnp.zeros((col_total, 2 * half_rank), jnp.float32)
        offset_grad, (sparse_blocks, row_grads) = lax.scan(one_block, start_grad, jnp.arange(block_total, dtype=jnp.int32))
        row_grads = row_grads.reshape(total_rows, 2 * half_rank)
        row_step = row_grads / (jnp.concatenate([right_norm, right_norm]) + epsilon)
        left_next = left_factor + jnp.zeros_like(left_factor).at[destination].set(row_step)
        right_factor = right_factor + offset_grad / (jnp.concatenate([left_norm, left_norm]) + epsilon)
        left_factor = left_next
    sparse = jnp.transpose(sparse_blocks, (1, 0, 2, 3)).reshape(2, total_rows, col_total).astype(jnp.bfloat16)
    return (sparse, left_factor, right_factor)
```

```python
from functools import partial

import jax
import jax.numpy as jnp
from jax import lax
from jax.experimental import pallas as pl
from jax.experimental.pallas import tpu as pltpu
from jax.sharding import PartitionSpec as P

epsilon = 1e-06
F32 = jnp.float32
BF16 = jnp.bfloat16


def turned(rows):
    half = rows.shape[1] // 2
    return jnp.concatenate([rows[:, half:], -rows[:, :half]], 1)


def unturned(rows):
    half = rows.shape[1] // 2
    return jnp.concatenate([-rows[:, half:], rows[:, :half]], 1)


def both_halves(norm):
    half = norm.shape[1] // 2
    once = norm[:, :half] + norm[:, half:]
    return jnp.concatenate([once, once], 1)


def residual_of(piece, model, inside, level):
    rows = inside.shape[0]
    real = jnp.where(inside, piece[0].astype(F32) - model[:rows], 0.0)
    imag = jnp.where(inside, piece[1].astype(F32) - model[rows:], 0.0)
    kept = level * lax.rsqrt(jnp.maximum(real * real + imag * imag, level * level))
    return real, imag, kept


def live_mask(begin, end, first_col, count):
    column = first_col + lax.broadcasted_iota(jnp.int32, (begin.shape[0], count), 1)
    return (column >= begin) & (column < end)


def rows_body(base_ref, piece_ref, left_ref, right_ref, level_ref, begin_ref, end_ref, grad_ref, norm_ref, acc_ref):
    step = pl.program_id(0)
    rows = left_ref.shape[0]
    cols = right_ref.shape[0]

    @pl.when(step == 0)
    def _():
        acc_ref[...] = jnp.zeros_like(acc_ref)
        norm_ref[...] = jnp.zeros_like(norm_ref)

    low = left_ref[...].astype(BF16)
    pair = jnp.concatenate([low, turned(low)], 0)
    right = right_ref[...]
    right_low = right.astype(BF16)
    model = lax.dot_general(pair, right_low, (((1,), (1,)), ((), ())), preferred_element_type=F32)
    inside = live_mask(begin_ref[...], end_ref[...], base_ref[0] + step * cols, cols)
    real, imag, kept = residual_of(piece_ref, model, inside, level_ref[...])
    error = jnp.concatenate([(real * kept).astype(BF16), (imag * kept).astype(BF16)], 0)
    acc_ref[...] += jnp.dot(error, right_low, preferred_element_type=F32)
    norm_ref[...] += jnp.sum(right * right, 0, keepdims=True)

    @pl.when(step == pl.num_programs(0) - 1)
    def _():
        grad_ref[...] = acc_ref[:rows] + unturned(acc_ref[rows:])


def cols_body(with_step, base_ref, piece_ref, left_ref, *refs):
    if with_step:
        move_ref, right_ref, level_ref, begin_ref, end_ref, next_ref, norm_ref, part_ref, acc_ref, left_norm_ref = refs
    else:
        right_ref, level_ref, begin_ref, end_ref, next_ref, norm_ref, acc_ref, left_norm_ref = refs
    step = pl.program_id(0)
    rows = left_ref.shape[0]
    cols = right_ref.shape[0]

    @pl.when(step == 0)
    def _():
        acc_ref[...] = jnp.zeros_like(acc_ref)
        left_norm_ref[...] = jnp.zeros_like(left_norm_ref)

    left = left_ref[...]
    if with_step:
        left = left + move_ref[...].astype(F32)
    low = left.astype(BF16)
    pair = jnp.concatenate([low, turned(low)], 0)
    right_low = right_ref[...].astype(BF16)
    model = lax.dot_general(pair, right_low, (((1,), (1,)), ((), ())), preferred_element_type=F32)
    inside = live_mask(begin_ref[...], end_ref[...], base_ref[0], cols)
    real, imag, kept = residual_of(piece_ref, model, inside, level_ref[...])
    error = jnp.concatenate([(real * kept).astype(BF16), (imag * kept).astype(BF16)], 0)
    acc_ref[...] += lax.dot_general(pair, error, (((0,), (0,)), ((), ())), preferred_element_type=F32)
    left_norm_ref[...] += jnp.sum(left * left, 0, keepdims=True)
    if with_step:
        part = jnp.dot(error, right_low, preferred_element_type=F32)
        part_ref[...] = part[:rows] + unturned(part[rows:])

    @pl.when(step == pl.num_programs(0) - 1)
    def _():
        right = right_ref[...]
        norm_ref[...] = jnp.sum(right * right, 0, keepdims=True)
        next_ref[...] = right + acc_ref[...].T / (both_halves(left_norm_ref[...]) + epsilon)


def sparse_body(base_ref, piece_ref, left_ref, right_ref, level_ref, begin_ref, end_ref, out_ref):
    step = pl.program_id(0)
    cols = right_ref.shape[0]
    low = left_ref[...].astype(BF16)
    pair = jnp.concatenate([low, turned(low)], 0)
    model = lax.dot_general(pair, right_ref[...], (((1,), (1,)), ((), ())), preferred_element_type=F32)
    inside = live_mask(begin_ref[...], end_ref[...], base_ref[0] + step * cols, cols)
    real, imag, kept = residual_of(piece_ref, model, inside, level_ref[...])
    out_ref[0] = (real - real * kept).astype(BF16)
    out_ref[1] = (imag - imag * kept).astype(BF16)


def col_block(count):
    block = min(512, count)
    while count % block:
        block //= 2
    return block


def whole(shape):
    return pl.BlockSpec(shape, lambda i, base: (0,) * len(shape))


def row_pass(base, pieces, left, right, level, begin, end):
    _, rows, cols = pieces.shape
    width = right.shape[1]
    block = col_block(cols)
    return pl.pallas_call(
        rows_body,
        grid_spec=pltpu.PrefetchScalarGridSpec(
            num_scalar_prefetch=1,
            grid=(cols // block,),
            in_specs=[
                pl.BlockSpec((2, rows, block), lambda i, base: (0, 0, i)),
                whole((rows, width)),
                pl.BlockSpec((block, width), lambda i, base: (i, 0)),
                pl.BlockSpec((1, block), lambda i, base: (0, i)),
                whole((rows, 1)),
                whole((rows, 1)),
            ],
            out_specs=[whole((rows, width)), whole((1, width))],
            scratch_shapes=[pltpu.VMEM((2 * rows, width), F32)],
        ),
        out_shape=[jax.ShapeDtypeStruct((rows, width), F32), jax.ShapeDtypeStruct((1, width), F32)],
        name="row_pass",
    )(base, pieces, left, right, level, begin, end)


def col_pass(base, turned_pieces, left, move, right, level, begin, end):
    count, _, rows, cols = turned_pieces.shape
    width = right.shape[1]
    by_block = pl.BlockSpec((rows, width), lambda i, base: (i, 0))
    ends = pl.BlockSpec((rows, 1), lambda i, base: (i, 0))
    with_step = move is not None
    return pl.pallas_call(
        partial(cols_body, with_step),
        grid_spec=pltpu.PrefetchScalarGridSpec(
            num_scalar_prefetch=1,
            grid=(count,),
            in_specs=[pl.BlockSpec((None, 2, rows, cols), lambda i, base: (i, 0, 0, 0)), by_block]
            + [by_block] * with_step
            + [whole((cols, width)), whole((1, cols)), ends, ends],
            out_specs=[whole((cols, width)), whole((1, width))] + [by_block] * with_step,
            scratch_shapes=[pltpu.VMEM((width, cols), F32), pltpu.VMEM((1, width), F32)],
        ),
        out_shape=[jax.ShapeDtypeStruct((cols, width), F32), jax.ShapeDtypeStruct((1, width), F32)]
        + [jax.ShapeDtypeStruct((count * rows, width), F32)] * with_step,
        name="col_pass_2" if with_step else "col_pass_1",
    )(base, turned_pieces, left, *([move] if with_step else []), right, level, begin, end)


def sparse_pass(base, pieces, left, right, level, begin, end):
    _, rows, cols = pieces.shape
    width = right.shape[1]
    block = col_block(cols)
    tall = pl.BlockSpec((2, rows, block), lambda i, base: (0, 0, i))
    return pl.pallas_call(
        sparse_body,
        grid_spec=pltpu.PrefetchScalarGridSpec(
            num_scalar_prefetch=1,
            grid=(cols // block,),
            in_specs=[
                tall,
                whole((rows, width)),
                pl.BlockSpec((block, width), lambda i, base: (i, 0)),
                pl.BlockSpec((1, block), lambda i, base: (0, i)),
                whole((rows, 1)),
                whole((rows, 1)),
            ],
            out_specs=tall,
        ),
        out_shape=jax.ShapeDtypeStruct(pieces.shape, BF16),
        name="sparse_pass",
    )(base, pieces, left, right, level, begin, end)


def exchange(blocks):
    return lax.all_to_all(blocks, "wide", split_axis=0, concat_axis=0, tiled=True)


def gather(block):
    return exchange(jnp.broadcast_to(block[None], (lax.axis_size("wide"),) + block.shape))


def swap_narrow(value):
    count = lax.axis_size("narrow")
    total = value
    for shift in range(1, count):
        total = total + lax.ppermute(value, "narrow", [(i, (i + shift) % count) for i in range(count)])
    return total


def as_rows(values, width):
    rows = -(-values.shape[0] // (8 * width)) * 8
    return jnp.pad(values, (0, rows * width - values.shape[0])).reshape(rows, width)


def local(pieces, destination, first_offset, valid_length, midpoint_factor, offset_factor, threshold):
    count = lax.axis_size("wide")
    _, rows, cols = pieces.shape
    width = offset_factor.shape[1]
    part = cols // count
    me = lax.axis_index("wide")
    base = lax.axis_index("narrow") * cols
    base_all = jnp.full((1,), base, jnp.int32)
    base_part = jnp.full((1,), base + me * part, jnp.int32)
    level = threshold[None, :]

    numbers = jnp.concatenate([destination, first_offset, first_offset + valid_length]).astype(F32)
    header = jnp.concatenate([midpoint_factor, as_rows(numbers, width)], 0)
    headers = gather(header)
    blocks = exchange(jnp.transpose(pieces.reshape(2, rows, count, part), (2, 0, 1, 3)))

    all_rows = headers[:, :rows].reshape(count * rows, width)
    tables = headers[:, rows:].reshape(count, -1)[:, : 3 * rows].astype(jnp.int32).reshape(count, 3, rows)
    dest_all = tables[:, 0].reshape(-1)
    begin_all = tables[:, 1].reshape(-1, 1)
    end_all = tables[:, 2].reshape(-1, 1)
    left_all = jnp.take(all_rows, dest_all, axis=0)
    left_mine = lax.dynamic_slice_in_dim(left_all, me * rows, rows, 0)
    begin = first_offset[:, None]
    end = begin + valid_length[:, None]

    grad, norm = row_pass(base_all, pieces, left_mine, offset_factor, level, begin, end)
    summed = swap_narrow(jnp.concatenate([grad, jnp.broadcast_to(norm, (8, width))], 0))
    move_mine = (summed[:rows] / (both_halves(summed[rows : rows + 1]) + epsilon)).astype(BF16)
    move_all = gather(move_mine).reshape(count * rows, width)

    right_part = lax.dynamic_slice_in_dim(offset_factor, me * part, part, 0)
    level_part = lax.dynamic_slice_in_dim(level, me * part, part, 1)
    right_one, _ = col_pass(base_part, blocks, left_all, None, right_part, level_part, begin_all, end_all)
    right_low = right_one.astype(BF16)
    low_all = gather(right_low).reshape(cols, width)

    right_two, norm_one, row_part = col_pass(
        base_part, blocks, left_all, move_all, right_one, level_part, begin_all, end_all
    )
    change_all = gather((right_two - right_low.astype(F32)).astype(BF16)).reshape(cols, width)

    segment_of = jnp.sum(
        jnp.where(
            dest_all[None, :] == jnp.arange(count * rows, dtype=jnp.int32)[:, None],
            jnp.arange(count * rows, dtype=jnp.int32)[None, :],
            0,
        ),
        1,
    )
    norm_high = norm_one.astype(BF16)
    norm_low = (norm_one - norm_high.astype(F32)).astype(BF16)
    norm_rows = jnp.concatenate([norm_high, norm_low, jnp.zeros((6, width), BF16)], 0)
    outgoing = jnp.concatenate(
        [
            jnp.take(row_part, segment_of, axis=0).astype(BF16).reshape(count, rows, width),
            jnp.broadcast_to(norm_rows[None], (count,) + norm_rows.shape),
        ],
        1,
    )
    summed = swap_narrow(jnp.sum(exchange(outgoing).astype(F32), 0))
    norm_two = both_halves(summed[rows : rows + 1] + summed[rows + 1 : rows + 2])
    my_segments = lax.dynamic_slice_in_dim(segment_of, me * rows, rows, 0)
    new_midpoint = (
        midpoint_factor + jnp.take(move_all, my_segments, axis=0).astype(F32) + summed[:rows] / (norm_two + epsilon)
    )

    left_mine = left_mine + move_mine.astype(F32)
    sparse = sparse_pass(base_all, pieces, left_mine, low_all, level, begin, end)
    new_offset = low_all.astype(F32) + change_all.astype(F32)
    return sparse, new_midpoint, new_offset


def solution(mesh):
    placed = (
        P(None, ("groups", "wide"), "narrow"),
        P("wide"),
        P("wide"),
        P("wide"),
        P(("groups", "wide"), None),
        P(("groups", "narrow"), None),
        P(("groups", "narrow")),
    )
    return jax.shard_map(
        local,
        mesh=mesh,
        in_specs=placed,
        out_specs=(
            P(None, ("groups", "wide"), "narrow"),
            P(("groups", "wide"), None),
            P(("groups", "narrow"), None),
        ),
        check_vma=False,
    )
```

```python
from functools import partial

import jax
import jax.numpy as jnp
from jax import lax
from jax.experimental import pallas as pl
from jax.experimental.pallas import tpu as pltpu
from jax.sharding import PartitionSpec as P

epsilon = 1e-06
F32 = jnp.float32
BF16 = jnp.bfloat16
PAD = 8
NEAR = 2


def turned(rows):
    half = rows.shape[1] // 2
    return jnp.concatenate([rows[:, half:], -rows[:, :half]], 1)


def unturned(rows):
    half = rows.shape[1] // 2
    return jnp.concatenate([-rows[:, half:], rows[:, :half]], 1)


def both_halves(norm):
    half = norm.shape[1] // 2
    once = norm[:, :half] + norm[:, half:]
    return jnp.concatenate([once, once], 1)


def parts_of(piece_real, piece_imag, left_low, right_low, level):
    rows = left_low.shape[0]
    pair = jnp.concatenate([left_low, turned(left_low)], 0)
    model = lax.dot_general(pair, right_low, (((1,), (1,)), ((), ())), preferred_element_type=F32)
    real = piece_real.astype(F32) - model[:rows]
    imag = piece_imag.astype(F32) - model[rows:]
    kept = level * lax.rsqrt(jnp.maximum(real * real + imag * imag, level * level))
    return pair, real, imag, kept


def live_mask(begin, end, first_col, count):
    column = lax.broadcasted_iota(jnp.int32, (begin.shape[0], count), 1)
    return (column >= begin - first_col) & (column < end - first_col)


def masked_error(real, imag, kept, inside):
    share = jnp.where(inside, kept, 0.0)
    return jnp.concatenate([(real * share).astype(BF16), (imag * share).astype(BF16)], 0)


def header_body(rows_ref, dest_ref, first_ref, valid_ref, out_ref):
    count, tall, width = out_ref.shape
    rows = tall - PAD
    first = first_ref[...]
    top = jnp.concatenate([dest_ref[...], first], 1).astype(F32)
    end = (first + valid_ref[...]).astype(F32)
    low = jnp.concatenate([end, jnp.zeros_like(end)], 1)
    numbers = jnp.concatenate([top, low, jnp.zeros((PAD - 2, width), F32)], 0)
    for target in range(count):
        out_ref[target, :rows] = rows_ref[...]
        out_ref[target, rows:] = numbers


def split_body(target_ref, piece_ref, *out_refs):
    cols = out_refs[0].shape[2]
    for index, out_ref in enumerate(out_refs):
        start = pl.multiple_of(target_ref[index] * cols, cols)
        out_ref[...] = piece_ref[:, :, pl.ds(start, cols)]


def rows_body(base_ref, piece_ref, left_ref, right_ref, level_ref, begin_ref, end_ref, grad_ref, acc_ref, norm_ref):
    step = pl.program_id(0)
    rows = left_ref.shape[0]
    cols = right_ref.shape[0]

    @pl.when(step == 0)
    def _():
        acc_ref[...] = jnp.zeros_like(acc_ref)
        norm_ref[...] = jnp.zeros_like(norm_ref)

    right = right_ref[...]
    right_low = right.astype(BF16)
    _, real, imag, kept = parts_of(piece_ref[0], piece_ref[1], left_ref[...].astype(BF16), right_low, level_ref[...])
    inside = live_mask(begin_ref[...], end_ref[...], base_ref[0] + step * cols, cols)
    error = masked_error(real, imag, kept, inside)
    acc_ref[...] += jnp.dot(error, right_low, preferred_element_type=F32)
    norm_ref[...] += jnp.sum(right * right, 0, keepdims=True)

    @pl.when(step == pl.num_programs(0) - 1)
    def _():
        grad_ref[:rows] = acc_ref[:rows] + unturned(acc_ref[rows:])
        grad_ref[rows:] = jnp.broadcast_to(norm_ref[...], (PAD, norm_ref.shape[1]))


def step_body(mine_ref, *refs):
    *other_refs, move_ref, out_ref = refs
    total = mine_ref[...]
    for other_ref in other_refs:
        total = total + other_ref[...]
    rows = total.shape[0] - PAD
    move = (total[:rows] / (both_halves(total[rows : rows + 1]) + epsilon)).astype(BF16)
    move_ref[...] = move
    for target in range(out_ref.shape[0]):
        out_ref[target] = move


def cols_body(counts, second, base_ref, source_ref, *refs):
    piece_refs, refs = refs[: len(counts)], refs[len(counts) :]
    if second:
        left_ref, move_ref, header_ref, right_ref, level_ref, change_ref, out_ref, acc_ref, part_ref = refs
    else:
        left_ref, header_ref, right_ref, level_ref, next_ref, low_ref, acc_ref = refs
    sources, tall, width = header_ref.shape
    rows = tall - PAD
    cols = right_ref.shape[0]
    right = right_ref[...]
    right_low = right.astype(BF16)
    level = level_ref[...]
    acc_ref[...] = jnp.zeros_like(acc_ref)
    if second:
        part_ref[...] = jnp.zeros_like(part_ref)

    def one(piece_real, piece_imag, source):
        at = pl.ds(pl.multiple_of(source * rows, rows), rows)
        left = left_ref[at, :]
        if second:
            left = left + move_ref[at, :].astype(F32)
        numbers = header_ref[source, rows:, :]
        standing = numbers.T.astype(jnp.int32)
        begin = standing[rows : 2 * rows, 0:1]
        end = standing[:rows, 1:2]
        pair, real, imag, kept = parts_of(piece_real, piece_imag, left.astype(BF16), right_low, level)
        error = masked_error(real, imag, kept, live_mask(begin, end, base_ref[0], cols))
        acc_ref[...] += lax.dot_general(pair, error, (((0,), (0,)), ((), ())), preferred_element_type=F32)
        if second:
            part = jnp.dot(error, right_low, preferred_element_type=F32)
            part = (part[:rows] + unturned(part[rows:])).astype(BF16)
            named = numbers[0:1, :rows].astype(jnp.int32)
            row = lax.broadcasted_iota(jnp.int32, (sources * rows, rows), 0)
            place = jnp.where(row == named, 1.0, 0.0).astype(BF16)
            part_ref[...] += jnp.dot(place, part, preferred_element_type=F32)

    index = 0
    for count, piece_ref in zip(counts, piece_refs):
        if count == 1:
            one(piece_ref[0], piece_ref[1], source_ref[index])
        else:

            @pl.loop(0, count)
            def _(slot, piece_ref=piece_ref, index=index):
                one(piece_ref[slot, 0], piece_ref[slot, 1], source_ref[index + slot])

        index += count

    left = left_ref[...]
    if second:
        left = left + move_ref[...].astype(F32)
    left_norm = both_halves(jnp.sum(left * left, 0, keepdims=True))
    after = right + acc_ref[...].T / (left_norm + epsilon)
    if not second:
        next_ref[...] = after
        low_ref[...] = after.astype(BF16)
        return
    change_ref[...] = (after - right_low.astype(F32)).astype(BF16)
    norm = jnp.sum(right * right, 0, keepdims=True)
    high = norm.astype(BF16).astype(F32)
    tail = jnp.concatenate([high, norm - high, jnp.zeros((PAD - 2, width), F32)], 0).astype(BF16)
    for target in range(sources):
        out_ref[target, :rows] = part_ref[target * rows : (target + 1) * rows].astype(BF16)
        out_ref[target, rows:] = tail


def sparse_body(counts, base_ref, source_ref, piece_ref, left_ref, move_ref, level_ref, begin_ref, end_ref, *refs):
    right_refs, out_ref = refs[:-1], refs[-1]
    low = (left_ref[...] + move_ref[...].astype(F32)).astype(BF16)
    begin = begin_ref[...]
    end = end_ref[...]

    def one(right, source):
        cols = right.shape[0]
        start = source * cols
        at = pl.ds(pl.multiple_of(start, cols), cols)
        _, real, imag, kept = parts_of(piece_ref[0, :, at], piece_ref[1, :, at], low, right, level_ref[:, at])
        share = jnp.where(live_mask(begin, end, base_ref[0] + start, cols), 1.0 - kept, 0.0)
        out_ref[0, :, at] = (real * share).astype(BF16)
        out_ref[1, :, at] = (imag * share).astype(BF16)

    index = 0
    for count, right_ref in zip(counts, right_refs):
        if count == 1:
            one(right_ref[...], source_ref[index])
        else:
            wide = max(1, 128 // right_ref.shape[1])
            block = wide * right_ref.shape[1]

            @pl.loop(0, count // wide)
            def _(slot, right_ref=right_ref):
                one(right_ref[pl.ds(slot * wide, wide)].reshape(block, right_ref.shape[2]), slot)

        index += count


def join_body(counts, source_ref, *refs):
    low_refs, change_refs, out_ref = refs[: len(counts)], refs[len(counts) : -1], refs[-1]
    index = 0
    for count, low_ref, change_ref in zip(counts, low_refs, change_refs):
        if count == 1:
            cols = low_ref.shape[0]
            at = pl.ds(pl.multiple_of(source_ref[index] * cols, cols), cols)
            out_ref[at, :] = low_ref[...].astype(F32) + change_ref[...].astype(F32)
        else:
            total = low_ref[...].astype(F32) + change_ref[...].astype(F32)
            out_ref[...] = total.reshape(out_ref.shape)
        index += count


VMEM = pl.BlockSpec(memory_space=pltpu.VMEM)
SMEM = pl.BlockSpec(memory_space=pltpu.SMEM)


def call(body, name, shapes, scalars, arrays, scratch=()):
    return pl.pallas_call(
        body,
        in_specs=[SMEM] * len(scalars) + [VMEM] * len(arrays),
        out_specs=jax.tree.map(lambda _: VMEM, shapes),
        out_shape=shapes,
        scratch_shapes=list(scratch),
        name=name,
    )(*scalars, *arrays)


def row_pass(base, pieces, left, right, level, begin, end):
    _, rows, cols = pieces.shape
    width = right.shape[1]
    block = min(512, cols)
    while cols % block:
        block //= 2

    def whole(*shape):
        return pl.BlockSpec(shape, lambda i, base: (0,) * len(shape))

    return pl.pallas_call(
        rows_body,
        grid_spec=pltpu.PrefetchScalarGridSpec(
            num_scalar_prefetch=1,
            grid=(cols // block,),
            in_specs=[
                pl.BlockSpec((2, rows, block), lambda i, base: (0, 0, i)),
                whole(rows, width),
                pl.BlockSpec((block, width), lambda i, base: (i, 0)),
                pl.BlockSpec((1, block), lambda i, base: (0, i)),
                whole(rows, 1),
                whole(rows, 1),
            ],
            out_specs=whole(rows + PAD, width),
            scratch_shapes=[pltpu.VMEM((2 * rows, width), F32), pltpu.VMEM((1, width), F32)],
        ),
        out_shape=jax.ShapeDtypeStruct((rows + PAD, width), F32),
        name="row_pass",
    )(base, pieces, left, right, level, begin, end)


def exchange(blocks):
    return lax.all_to_all(blocks, "wide", split_axis=0, concat_axis=0, tiled=True)


def other_narrow(value):
    count = lax.axis_size("narrow")
    return [lax.ppermute(value, "narrow", [(i, (i + k) % count) for i in range(count)]) for k in range(1, count)]


def small_wide():
    count = lax.axis_size("wide")
    return count % NEAR == 0 and count <= 4 * NEAR


def shift(value, far, near):
    outer = lax.axis_size("wide") // NEAR
    pairs = [
        (z * NEAR + x, (z + far) % outer * NEAR + (x + near) % NEAR) for z in range(outer) for x in range(NEAR)
    ]
    return lax.ppermute(value, "wide", pairs)


def device_at(far, near):
    outer = lax.axis_size("wide") // NEAR
    me = lax.axis_index("wide")
    return (me // NEAR + far) % outer * NEAR + (me % NEAR + near) % NEAR


def far_first(outer):
    return sorted(range(1, outer), key=lambda far: -min(far, outer - far))


def send_parts(pieces):
    count = lax.axis_size("wide")
    _, rows, cols = pieces.shape
    part = cols // count
    if not small_wide():
        blocks = exchange(jnp.transpose(pieces.reshape(2, rows, count, part), (2, 0, 1, 3)))
        return [blocks], (count,), jnp.arange(count, dtype=jnp.int32)
    outer = count // NEAR
    ways = [(far, near) for far in far_first(outer) for near in range(NEAR)] + [(0, near) for near in range(NEAR)]
    ways = [way for way in ways if way != (0, 0)] + [(0, 0)]
    targets = jnp.stack([device_at(*way) for way in ways]).astype(jnp.int32)
    shapes = [jax.ShapeDtypeStruct((2, rows, part), pieces.dtype)] * count
    parts = call(split_body, "split", shapes, [targets], [pieces])
    arrived = [block if way == (0, 0) else shift(block, *way) for way, block in zip(ways, parts)]
    sources = jnp.stack([device_at(-far, -near) for far, near in ways]).astype(jnp.int32)
    return arrived, (1,) * count, sources


def gather_parts(block):
    count = lax.axis_size("wide")
    if not small_wide():
        blocks = exchange(jnp.broadcast_to(block[None], (count,) + block.shape))
        return [blocks], (count,), jnp.arange(count, dtype=jnp.int32)
    outer = count // NEAR
    held = [(block, 0, 0)]
    held += [(shift(block, 0, near), 0, near) for near in range(1, NEAR)]
    for far in range(1, outer):
        arrived = shift(block, far, 0)
        held.append((arrived, far, 0))
        held += [(shift(arrived, 0, near), far, near) for near in range(1, NEAR)]
    sources = jnp.stack([device_at(-far, -near) for _, far, near in held]).astype(jnp.int32)
    return [value for value, _, _ in held], (1,) * count, sources


def local(pieces, destination, first_offset, valid_length, midpoint_factor, offset_factor, threshold):
    count = lax.axis_size("wide")
    _, rows, cols = pieces.shape
    width = offset_factor.shape[1]
    part = cols // count
    total = count * rows
    me = lax.axis_index("wide")
    base = lax.axis_index("narrow") * cols
    base_all = jnp.full((1,), base, jnp.int32)
    base_part = jnp.full((1,), base + me * part, jnp.int32)
    level = threshold[None, :]
    begin = first_offset[:, None]
    end = begin + valid_length[:, None]

    header = call(
        header_body,
        "header",
        jax.ShapeDtypeStruct((count, rows + PAD, width), F32),
        [],
        [midpoint_factor, destination[None], first_offset[None], valid_length[None]],
    )
    headers = exchange(header)
    blocks, block_counts, block_sources = send_parts(pieces)

    all_rows = headers[:, :rows].reshape(total, width)
    left_mine = jnp.take(all_rows, destination, axis=0)
    row_grad = row_pass(base_all, pieces, left_mine, offset_factor, level, begin, end)
    move_mine, moves = call(
        step_body,
        "step",
        [jax.ShapeDtypeStruct((rows, width), BF16), jax.ShapeDtypeStruct((count, rows, width), BF16)],
        [],
        [row_grad] + other_narrow(row_grad),
    )
    move_all = exchange(moves).reshape(total, width)

    dest_all = headers[:, rows, :rows].astype(jnp.int32).reshape(total)
    left_all = jnp.take(all_rows, dest_all, axis=0)
    right_part = lax.dynamic_slice_in_dim(offset_factor, me * part, part, 0)
    level_part = lax.dynamic_slice_in_dim(level, me * part, part, 1)
    right_one, right_low = call(
        partial(cols_body, block_counts, False),
        "col_pass_1",
        [jax.ShapeDtypeStruct((part, width), F32), jax.ShapeDtypeStruct((part, width), BF16)],
        [base_part, block_sources],
        [*blocks, left_all, headers, right_part, level_part],
        [pltpu.VMEM((width, part), F32)],
    )
    lows, counts, sources = gather_parts(right_low)

    change, outgoing = call(
        partial(cols_body, block_counts, True),
        "col_pass_2",
        [jax.ShapeDtypeStruct((part, width), BF16), jax.ShapeDtypeStruct((count, rows + PAD, width), BF16)],
        [base_part, block_sources],
        [*blocks, left_all, move_all, headers, right_one, level_part],
        [pltpu.VMEM((width, part), F32), pltpu.VMEM((total, width), F32)],
    )
    changes, _, _ = gather_parts(change)

    my_rows = me * rows + jnp.arange(rows, dtype=jnp.int32)
    order = jnp.arange(total, dtype=jnp.int32)
    my_segments = jnp.sum(jnp.where(dest_all[None, :] == my_rows[:, None], order[None, :], 0), 1)
    first_step = jnp.take(move_all, my_segments, axis=0).astype(F32)
    summed = jnp.sum(exchange(outgoing).astype(F32), 0)
    for other in other_narrow(summed):
        summed = summed + other
    norm_two = both_halves(summed[rows : rows + 1] + summed[rows + 1 : rows + 2])
    new_midpoint = midpoint_factor + first_step + summed[:rows] / (norm_two + epsilon)

    sparse = call(
        partial(sparse_body, counts),
        "sparse_pass",
        jax.ShapeDtypeStruct(pieces.shape, BF16),
        [base_all, sources],
        [pieces, left_mine, move_mine, level, begin, end, *lows],
    )
    new_offset = call(
        partial(join_body, counts),
        "join",
        jax.ShapeDtypeStruct((cols, width), F32),
        [sources],
        [*lows, *changes],
    )
    return sparse, new_midpoint, new_offset


def solution(mesh):
    placed = (
        P(None, ("groups", "wide"), "narrow"),
        P("wide"),
        P("wide"),
        P("wide"),
        P(("groups", "wide"), None),
        P(("groups", "narrow"), None),
        P(("groups", "narrow")),
    )
    return jax.shard_map(
        local,
        mesh=mesh,
        in_specs=placed,
        out_specs=(
            P(None, ("groups", "wide"), "narrow"),
            P(("groups", "wide"), None),
            P(("groups", "narrow"), None),
        ),
        check_vma=False,
    )
```

```python
from functools import partial

import jax
import jax.numpy as jnp
from jax import lax
from jax.experimental import pallas as pl
from jax.experimental.pallas import tpu as pltpu
from jax.sharding import PartitionSpec as P


epsilon = 1e-06
F32 = jnp.float32
BF16 = jnp.bfloat16
PAD = 8
NEAR = 2


def turned(rows):
    half = rows.shape[1] // 2
    return jnp.concatenate([rows[:, half:], -rows[:, :half]], 1)


def unturned(rows):
    half = rows.shape[1] // 2
    return jnp.concatenate([-rows[:, half:], rows[:, :half]], 1)


def both_halves(norm):
    half = norm.shape[1] // 2
    once = norm[:, :half] + norm[:, half:]
    return jnp.concatenate([once, once], 1)


def parts_of(piece_real, piece_imag, left_low, right_low, level):
    rows = left_low.shape[0]
    pair = jnp.concatenate([left_low, turned(left_low)], 0)
    model = lax.dot_general(pair, right_low, (((1,), (1,)), ((), ())), preferred_element_type=F32)
    real = piece_real.astype(F32) - model[:rows]
    imag = piece_imag.astype(F32) - model[rows:]
    kept = level * lax.rsqrt(jnp.maximum(real * real + imag * imag, level * level))
    return pair, real, imag, kept


def live_mask(begin, end, first_col, count):
    column = lax.broadcasted_iota(jnp.int32, (begin.shape[0], count), 1)
    return (column >= begin - first_col) & (column < end - first_col)


def masked_error(real, imag, kept, inside):
    share = jnp.where(inside, kept, 0.0)
    return jnp.concatenate([(real * share).astype(BF16), (imag * share).astype(BF16)], 0)


def header_body(rows_ref, dest_ref, first_ref, valid_ref, out_ref):
    count, tall, width = out_ref.shape
    rows = tall - PAD
    first = first_ref[...]
    top = jnp.concatenate([dest_ref[...], first], 1).astype(F32)
    end = (first + valid_ref[...]).astype(F32)
    low = jnp.concatenate([end, jnp.zeros_like(end)], 1)
    numbers = jnp.concatenate([top, low, jnp.zeros((PAD - 2, width), F32)], 0)
    for target in range(count):
        out_ref[target, :rows] = rows_ref[...]
        out_ref[target, rows:] = numbers


def split_body(target_ref, piece_ref, *out_refs):
    cols = out_refs[0].shape[2]
    for index, out_ref in enumerate(out_refs):
        start = pl.multiple_of(target_ref[index] * cols, cols)
        out_ref[...] = piece_ref[:, :, pl.ds(start, cols)]


def rows_body(base_ref, piece_ref, left_ref, right_ref, level_ref, begin_ref, end_ref, grad_ref, acc_ref, norm_ref):
    rows, width = left_ref.shape
    block = column_block(right_ref.shape[0])
    low = left_ref[...].astype(BF16)
    begin = begin_ref[...]
    end = end_ref[...]
    acc_ref[...] = jnp.zeros_like(acc_ref)
    norm_ref[...] = jnp.zeros_like(norm_ref)

    @pl.loop(0, right_ref.shape[0] // block)
    def _(step):
        start = step * block
        at = pl.ds(pl.multiple_of(start, block), block)
        right = right_ref[at, :]
        right_low = right.astype(BF16)
        _, real, imag, kept = parts_of(piece_ref[0, :, at], piece_ref[1, :, at], low, right_low, level_ref[:, at])
        error = masked_error(real, imag, kept, live_mask(begin, end, base_ref[0] + start, block))
        acc_ref[...] += jnp.dot(error, right_low, preferred_element_type=F32)
        norm_ref[...] += jnp.sum((right * right).reshape(-1, 8, width), 0)

    grad_ref[:rows] = acc_ref[:rows] + unturned(acc_ref[rows:])
    grad_ref[rows:] = jnp.broadcast_to(jnp.sum(norm_ref[...], 0, keepdims=True), (PAD, width))


def step_body(mine_ref, *refs):
    *other_refs, move_ref, out_ref = refs
    total = mine_ref[...]
    for other_ref in other_refs:
        total = total + other_ref[...]
    rows = total.shape[0] - PAD
    move = (total[:rows] / (both_halves(total[rows : rows + 1]) + epsilon)).astype(BF16)
    move_ref[...] = move
    for target in range(out_ref.shape[0]):
        out_ref[target] = move


def cols_body(counts, second, base_ref, source_ref, *refs):
    piece_refs, refs = refs[: len(counts)], refs[len(counts) :]
    if second:
        left_ref, move_ref, header_ref, right_ref, level_ref, change_ref, out_ref, acc_ref, part_ref = refs
    else:
        left_ref, header_ref, right_ref, level_ref, next_ref, low_ref, acc_ref = refs
    sources, tall, width = header_ref.shape
    rows = tall - PAD
    cols = right_ref.shape[0]
    right = right_ref[...]
    right_low = right.astype(BF16)
    level = level_ref[...]
    acc_ref[...] = jnp.zeros_like(acc_ref)
    if second:
        part_ref[...] = jnp.zeros_like(part_ref)

    def one(piece_real, piece_imag, source):
        at = pl.ds(pl.multiple_of(source * rows, rows), rows)
        left = left_ref[at, :]
        if second:
            left = left + move_ref[at, :].astype(F32)
        numbers = header_ref[source, rows:, :]
        standing = numbers.T.astype(jnp.int32)
        begin = standing[rows : 2 * rows, 0:1]
        end = standing[:rows, 1:2]
        pair, real, imag, kept = parts_of(piece_real, piece_imag, left.astype(BF16), right_low, level)
        error = masked_error(real, imag, kept, live_mask(begin, end, base_ref[0], cols))
        acc_ref[...] += lax.dot_general(pair, error, (((0,), (0,)), ((), ())), preferred_element_type=F32)
        if second:
            part = jnp.dot(error, right_low, preferred_element_type=F32)
            part = (part[:rows] + unturned(part[rows:])).astype(BF16)
            named = numbers[0:1, :rows].astype(jnp.int32)
            row = lax.broadcasted_iota(jnp.int32, (sources * rows, rows), 0)
            place = jnp.where(row == named, 1.0, 0.0).astype(BF16)
            part_ref[...] += jnp.dot(place, part, preferred_element_type=F32)

    index = 0
    for count, piece_ref in zip(counts, piece_refs):
        if count == 1:
            one(piece_ref[0], piece_ref[1], source_ref[index])
        else:

            @pl.loop(0, count)
            def _(slot, piece_ref=piece_ref, index=index):
                one(piece_ref[slot, 0], piece_ref[slot, 1], source_ref[index + slot])

        index += count

    left = left_ref[...]
    if second:
        left = left + move_ref[...].astype(F32)
    left_norm = both_halves(jnp.sum(left * left, 0, keepdims=True))
    after = right + acc_ref[...].T / (left_norm + epsilon)
    if not second:
        next_ref[...] = after
        low_ref[...] = after.astype(BF16)
        return
    change_ref[...] = (after - right_low.astype(F32)).astype(BF16)
    norm = jnp.sum(right * right, 0, keepdims=True)
    high = norm.astype(BF16).astype(F32)
    tail = jnp.concatenate([high, norm - high, jnp.zeros((PAD - 2, width), F32)], 0).astype(BF16)
    for target in range(sources):
        out_ref[target, :rows] = part_ref[target * rows : (target + 1) * rows].astype(BF16)
        out_ref[target, rows:] = tail


def sparse_body(counts, base_ref, source_ref, piece_ref, left_ref, move_ref, level_ref, begin_ref, end_ref, *refs):
    right_refs, out_ref = refs[:-1], refs[-1]
    low = (left_ref[...] + move_ref[...].astype(F32)).astype(BF16)
    begin = begin_ref[...]
    end = end_ref[...]

    def one(right, source):
        cols = right.shape[0]
        start = source * cols
        at = pl.ds(pl.multiple_of(start, cols), cols)
        _, real, imag, kept = parts_of(piece_ref[0, :, at], piece_ref[1, :, at], low, right, level_ref[:, at])
        share = jnp.where(live_mask(begin, end, base_ref[0] + start, cols), 1.0 - kept, 0.0)
        out_ref[0, :, at] = (real * share).astype(BF16)
        out_ref[1, :, at] = (imag * share).astype(BF16)

    index = 0
    for count, right_ref in zip(counts, right_refs):
        if count == 1:
            one(right_ref[...], source_ref[index])
        else:
            wide = max(1, 128 // right_ref.shape[1])
            block = wide * right_ref.shape[1]

            @pl.loop(0, count // wide)
            def _(slot, right_ref=right_ref):
                one(right_ref[pl.ds(slot * wide, wide)].reshape(block, right_ref.shape[2]), slot)

        index += count


def join_body(counts, source_ref, *refs):
    low_refs, change_refs, out_ref = refs[: len(counts)], refs[len(counts) : -1], refs[-1]
    index = 0
    for count, low_ref, change_ref in zip(counts, low_refs, change_refs):
        if count == 1:
            cols = low_ref.shape[0]
            at = pl.ds(pl.multiple_of(source_ref[index] * cols, cols), cols)
            out_ref[at, :] = low_ref[...].astype(F32) + change_ref[...].astype(F32)
        else:
            total = low_ref[...].astype(F32) + change_ref[...].astype(F32)
            out_ref[...] = total.reshape(out_ref.shape)
        index += count


VMEM = pl.BlockSpec(memory_space=pltpu.VMEM)
SMEM = pl.BlockSpec(memory_space=pltpu.SMEM)


def call(body, shapes, scalars, arrays, scratch=()):
    return pl.pallas_call(
        body,
        in_specs=[SMEM] * len(scalars) + [VMEM] * len(arrays),
        out_specs=jax.tree.map(lambda _: VMEM, shapes),
        out_shape=shapes,
        scratch_shapes=list(scratch),
    )(*scalars, *arrays)


def column_block(count):
    block = min(512, count)
    while count % block:
        block //= 2
    return block


def rows_at(table, index):
    return table.at[index].get(mode="promise_in_bounds")


def exchange(blocks):
    return lax.all_to_all(blocks, "wide", split_axis=0, concat_axis=0, tiled=True)


def other_narrow(value):
    count = lax.axis_size("narrow")
    return [lax.ppermute(value, "narrow", [(i, (i + k) % count) for i in range(count)]) for k in range(1, count)]


def small_wide():
    count = lax.axis_size("wide")
    return count % NEAR == 0 and count <= 4 * NEAR


def shift(value, far, near):
    outer = lax.axis_size("wide") // NEAR
    pairs = [
        (z * NEAR + x, (z + far) % outer * NEAR + (x + near) % NEAR) for z in range(outer) for x in range(NEAR)
    ]
    return lax.ppermute(value, "wide", pairs)


def device_at(far, near):
    outer = lax.axis_size("wide") // NEAR
    me = lax.axis_index("wide")
    return (me // NEAR + far) % outer * NEAR + (me % NEAR + near) % NEAR


def far_first(outer):
    return sorted(range(1, outer), key=lambda far: -min(far, outer - far))


def send_parts(pieces):
    count = lax.axis_size("wide")
    _, rows, cols = pieces.shape
    part = cols // count
    if not small_wide():
        blocks = exchange(jnp.transpose(pieces.reshape(2, rows, count, part), (2, 0, 1, 3)))
        return [blocks], (count,), jnp.arange(count, dtype=jnp.int32)
    outer = count // NEAR
    ways = [(far, near) for far in far_first(outer) for near in range(NEAR)] + [(0, near) for near in range(NEAR)]
    ways = [way for way in ways if way != (0, 0)] + [(0, 0)]
    targets = jnp.stack([device_at(*way) for way in ways]).astype(jnp.int32)
    shapes = [jax.ShapeDtypeStruct((2, rows, part), pieces.dtype)] * count
    parts = call(split_body, shapes, [targets], [pieces])
    arrived = [block if way == (0, 0) else shift(block, *way) for way, block in zip(ways, parts)]
    sources = jnp.stack([device_at(-far, -near) for far, near in ways]).astype(jnp.int32)
    return arrived, (1,) * count, sources


def gather_parts(block):
    count = lax.axis_size("wide")
    if not small_wide():
        blocks = exchange(jnp.broadcast_to(block[None], (count,) + block.shape))
        return [blocks], (count,), jnp.arange(count, dtype=jnp.int32)
    outer = count // NEAR
    held = [(block, 0, 0)]
    held += [(shift(block, 0, near), 0, near) for near in range(1, NEAR)]
    first = [(shift(block, far, 0), far) for far in range(1, outer)]
    for arrived, far in first:
        held.append((arrived, far, 0))
        held += [(shift(arrived, 0, near), far, near) for near in range(1, NEAR)]
    sources = jnp.stack([device_at(-far, -near) for _, far, near in held]).astype(jnp.int32)
    return [value for value, _, _ in held], (1,) * count, sources


def body(pieces, destination, first_offset, valid_length, midpoint_factor, offset_factor, threshold):
    count = lax.axis_size("wide")
    _, rows, cols = pieces.shape
    width = offset_factor.shape[1]
    part = cols // count
    total = count * rows
    me = lax.axis_index("wide")
    base = lax.axis_index("narrow") * cols
    base_all = jnp.full((1,), base, jnp.int32)
    base_part = jnp.full((1,), base + me * part, jnp.int32)
    level = threshold[None, :]
    begin = first_offset[:, None]
    end = begin + valid_length[:, None]

    header = call(
        header_body,
        jax.ShapeDtypeStruct((count, rows + PAD, width), F32),
        [],
        [midpoint_factor, destination[None], first_offset[None], valid_length[None]],
    )
    headers = exchange(header)
    blocks, block_counts, block_sources = send_parts(pieces)

    all_rows = headers[:, :rows].reshape(total, width)
    left_mine = rows_at(all_rows, destination)
    row_grad = call(
        rows_body,
        jax.ShapeDtypeStruct((rows + PAD, width), F32),
        [base_all],
        [pieces, left_mine, offset_factor, level, begin, end],
        [pltpu.VMEM((2 * rows, width), F32), pltpu.VMEM((8, width), F32)],
    )
    move_mine, moves = call(
        step_body,
        [jax.ShapeDtypeStruct((rows, width), BF16), jax.ShapeDtypeStruct((count, rows, width), BF16)],
        [],
        [row_grad] + other_narrow(row_grad),
    )
    move_all = exchange(moves).reshape(total, width)

    dest_all = headers[:, rows, :rows].astype(jnp.int32).reshape(total)
    left_all = rows_at(all_rows, dest_all)
    right_part = lax.dynamic_slice_in_dim(offset_factor, me * part, part, 0)
    level_part = lax.dynamic_slice_in_dim(level, me * part, part, 1)
    right_one, right_low = call(
        partial(cols_body, block_counts, False),
        [jax.ShapeDtypeStruct((part, width), F32), jax.ShapeDtypeStruct((part, width), BF16)],
        [base_part, block_sources],
        [*blocks, left_all, headers, right_part, level_part],
        [pltpu.VMEM((width, part), F32)],
    )
    lows, counts, sources = gather_parts(right_low)

    change, outgoing = call(
        partial(cols_body, block_counts, True),
        [jax.ShapeDtypeStruct((part, width), BF16), jax.ShapeDtypeStruct((count, rows + PAD, width), BF16)],
        [base_part, block_sources],
        [*blocks, left_all, move_all, headers, right_one, level_part],
        [pltpu.VMEM((width, part), F32), pltpu.VMEM((total, width), F32)],
    )
    changes, _, _ = gather_parts(change)

    my_rows = me * rows + jnp.arange(rows, dtype=jnp.int32)
    order = jnp.arange(total, dtype=jnp.int32)
    my_segments = jnp.sum(jnp.where(dest_all[None, :] == my_rows[:, None], order[None, :], 0), 1)
    first_step = rows_at(move_all, my_segments).astype(F32)
    arrived = exchange(outgoing)
    summed = jnp.sum(arrived.astype(F32), 0)
    for other in other_narrow(summed):
        summed = summed + other
    norm_two = both_halves(summed[rows : rows + 1] + summed[rows + 1 : rows + 2])
    new_midpoint = midpoint_factor + first_step + summed[:rows] / (norm_two + epsilon)

    sparse = call(
        partial(sparse_body, counts),
        jax.ShapeDtypeStruct(pieces.shape, BF16),
        [base_all, sources],
        [pieces, left_mine, move_mine, level, begin, end, *lows],
    )
    new_offset = call(
        partial(join_body, counts), jax.ShapeDtypeStruct((cols, width), F32), [sources], [*lows, *changes]
    )
    return sparse, new_midpoint, new_offset


def solution(mesh):
    placed = (
        P(None, ("groups", "wide"), "narrow"),
        P("wide"),
        P("wide"),
        P("wide"),
        P(("groups", "wide"), None),
        P(("groups", "narrow"), None),
        P(("groups", "narrow")),
    )
    return jax.shard_map(
        body,
        mesh=mesh,
        in_specs=placed,
        out_specs=(
            P(None, ("groups", "wide"), "narrow"),
            P(("groups", "wide"), None),
            P(("groups", "narrow"), None),
        ),
        check_vma=False,
    )
```

```python
from functools import partial

import jax
import jax.numpy as jnp
from jax import lax
from jax.experimental import pallas as pl
from jax.experimental.pallas import tpu as pltpu
from jax.sharding import PartitionSpec as P


epsilon = 1e-06
F32 = jnp.float32
BF16 = jnp.bfloat16
PAD = 8
NEAR = 2


def turned(rows):
    half = rows.shape[1] // 2
    return jnp.concatenate([rows[:, half:], -rows[:, :half]], 1)


def unturned(rows):
    half = rows.shape[1] // 2
    return jnp.concatenate([-rows[:, half:], rows[:, :half]], 1)


def both_halves(norm):
    half = norm.shape[1] // 2
    once = norm[:, :half] + norm[:, half:]
    return jnp.concatenate([once, once], 1)


def parts_of(piece_real, piece_imag, left_low, right_low, level):
    rows = left_low.shape[0]
    pair = jnp.concatenate([left_low, turned(left_low)], 0)
    model = lax.dot_general(pair, right_low, (((1,), (1,)), ((), ())), preferred_element_type=F32)
    real = piece_real.astype(F32) - model[:rows]
    imag = piece_imag.astype(F32) - model[rows:]
    kept = level * lax.rsqrt(jnp.maximum(real * real + imag * imag, level * level))
    return pair, real, imag, kept


def live_mask(begin, end, first_col, count):
    column = lax.broadcasted_iota(jnp.int32, (begin.shape[0], count), 1)
    return (column >= begin - first_col) & (column < end - first_col)


def masked_error(real, imag, kept, inside):
    share = jnp.where(inside, kept, 0.0)
    return jnp.concatenate([(real * share).astype(BF16), (imag * share).astype(BF16)], 0)


def row_numbers(dest_ref, first_ref, valid_ref, width):
    first = first_ref[...]
    top = jnp.concatenate([dest_ref[...], first], 1).astype(F32)
    end = (first + valid_ref[...]).astype(F32)
    low = jnp.concatenate([end, jnp.zeros_like(end)], 1)
    return jnp.concatenate([top, low, jnp.zeros((PAD - 2, width), F32)], 0)


def standing_numbers(numbers, rows):
    columns = numbers.T.astype(jnp.int32)
    return columns[:rows, 0:1], columns[rows : 2 * rows, 0:1], columns[:rows, 1:2]


def three_ways(table):
    high = table.astype(BF16)
    rest = table - high.astype(F32)
    middle = rest.astype(BF16)
    return [high, middle, (rest - middle.astype(F32)).astype(BF16)]


def picked(dest, ways):
    row = lax.broadcasted_iota(jnp.int32, (dest.shape[0], ways[0].shape[0]), 1)
    place = jnp.where(row == dest, 1.0, 0.0).astype(BF16)
    parts = [jnp.dot(place, way, preferred_element_type=F32) for way in ways]
    return parts[0] + parts[1] + parts[2]


def prep_body(ways, rows_ref, dest_ref, first_ref, valid_ref, *refs):
    piece_ref, header_ref, numbers_ref, *part_refs = refs if ways else (None, *refs)
    count, tall, width = header_ref.shape
    rows = tall - PAD
    numbers = row_numbers(dest_ref, first_ref, valid_ref, width)
    numbers_ref[...] = numbers
    for target in range(count):
        header_ref[target, :rows] = rows_ref[...]
        header_ref[target, rows:] = numbers
    for way, part_ref in zip(ways, part_refs):
        cols = part_ref.shape[2]
        part_ref[...] = piece_ref[:, :, pl.ds(pl.multiple_of(device_at(*way) * cols, cols), cols)]


def rows_body(piece_ref, header_ref, numbers_ref, right_ref, level_ref, *refs):
    grad_ref, left_ref, own_ref, acc_ref, norm_ref = refs
    rows, width = left_ref.shape
    cols = right_ref.shape[0]
    part = own_ref.shape[0]
    block = column_block(cols)
    base = lax.axis_index("narrow") * cols
    dest, begin, end = standing_numbers(numbers_ref[...], rows)
    left = picked(dest, three_ways(header_ref[:, :rows].reshape(-1, width)))
    left_ref[...] = left
    low = left.astype(BF16)
    own_ref[...] = right_ref[pl.ds(pl.multiple_of(lax.axis_index("wide") * part, part), part), :]
    acc_ref[...] = jnp.zeros_like(acc_ref)
    norm_ref[...] = jnp.zeros_like(norm_ref)

    @pl.loop(0, cols // block)
    def _(step):
        start = step * block
        at = pl.ds(pl.multiple_of(start, block), block)
        right = right_ref[at, :]
        right_low = right.astype(BF16)
        _, real, imag, kept = parts_of(piece_ref[0, :, at], piece_ref[1, :, at], low, right_low, level_ref[:, at])
        error = masked_error(real, imag, kept, live_mask(begin, end, base + start, block))
        acc_ref[...] += jnp.dot(error, right_low, preferred_element_type=F32)
        norm_ref[...] += jnp.sum((right * right).reshape(-1, 8, width), 0)

    grad_ref[:rows] = acc_ref[:rows] + unturned(acc_ref[rows:])
    grad_ref[rows:] = jnp.broadcast_to(jnp.sum(norm_ref[...], 0, keepdims=True), (PAD, width))


def step_body(mine_ref, *refs):
    *other_refs, move_ref, out_ref = refs
    total = mine_ref[...]
    for other_ref in other_refs:
        total = total + other_ref[...]
    rows = total.shape[0] - PAD
    move = (total[:rows] / (both_halves(total[rows : rows + 1]) + epsilon)).astype(BF16)
    move_ref[...] = move
    for target in range(out_ref.shape[0]):
        out_ref[target] = move


def cols_body(ways, second, header_ref, right_ref, level_ref, *refs):
    many = len(ways) or 1
    piece_refs, refs = refs[:many], refs[many:]
    if second:
        left_ref, move_ref, change_ref, out_ref, acc_ref, part_ref = refs
        part_ref[...] = jnp.zeros_like(part_ref)
    else:
        next_ref, low_ref, left_ref, acc_ref = refs
        table = three_ways(header_ref[:, : header_ref.shape[1] - PAD].reshape(-1, header_ref.shape[2]))
    sources, tall, width = header_ref.shape
    rows = tall - PAD
    part = right_ref.shape[0]
    right = right_ref[...]
    right_low = right.astype(BF16)
    me = lax.axis_index("wide")
    base = lax.axis_index("narrow") * (sources * part) + me * part
    if level_ref.shape[1] == part:
        level = level_ref[...]
    else:
        level = level_ref[:, pl.ds(pl.multiple_of(me * part, part), part)]
    acc_ref[...] = jnp.zeros_like(acc_ref)

    def one(piece_real, piece_imag, source):
        at = pl.ds(pl.multiple_of(source * rows, rows), rows)
        numbers = header_ref[source, rows:, :]
        dest, begin, end = standing_numbers(numbers, rows)
        if second:
            left = left_ref[at, :] + move_ref[at, :].astype(F32)
        else:
            left = picked(dest, table)
            left_ref[at, :] = left
        pair, real, imag, kept = parts_of(piece_real, piece_imag, left.astype(BF16), right_low, level)
        error = masked_error(real, imag, kept, live_mask(begin, end, base, part))
        acc_ref[...] += lax.dot_general(pair, error, (((0,), (0,)), ((), ())), preferred_element_type=F32)
        if second:
            grad = jnp.dot(error, right_low, preferred_element_type=F32)
            grad = (grad[:rows] + unturned(grad[rows:])).astype(BF16)
            named = numbers[0:1, :rows].astype(jnp.int32)
            row = lax.broadcasted_iota(jnp.int32, (sources * rows, rows), 0)
            place = jnp.where(row == named, 1.0, 0.0).astype(BF16)
            part_ref[...] += jnp.dot(place, grad, preferred_element_type=F32)

    for way, piece_ref in zip(ways, piece_refs):
        one(piece_ref[0], piece_ref[1], device_at(-way[0], -way[1]))
    if not ways:

        @pl.loop(0, sources)
        def _(source):
            one(piece_refs[0][source, 0], piece_refs[0][source, 1], source)

    left = left_ref[...]
    if second:
        left = left + move_ref[...].astype(F32)
    left_norm = both_halves(jnp.sum(left * left, 0, keepdims=True))
    after = right + acc_ref[...].T / (left_norm + epsilon)
    if not second:
        next_ref[...] = after
        low_ref[...] = after.astype(BF16)
        return
    change_ref[...] = (after - right_low.astype(F32)).astype(BF16)
    norm = jnp.sum(right * right, 0, keepdims=True)
    high = norm.astype(BF16).astype(F32)
    tail = jnp.concatenate([high, norm - high, jnp.zeros((PAD - 2, width), F32)], 0).astype(BF16)
    for target in range(sources):
        out_ref[target, :rows] = part_ref[target * rows : (target + 1) * rows].astype(BF16)
        out_ref[target, rows:] = tail


def sparse_body(ways, piece_ref, numbers_ref, left_ref, move_ref, level_ref, *refs):
    right_refs, out_ref = refs[:-1], refs[-1]
    low = (left_ref[...] + move_ref[...].astype(F32)).astype(BF16)
    _, begin, end = standing_numbers(numbers_ref[...], low.shape[0])
    base = lax.axis_index("narrow") * piece_ref.shape[2]

    def one(right, source):
        cols = right.shape[0]
        start = source * cols
        at = pl.ds(pl.multiple_of(start, cols), cols)
        _, real, imag, kept = parts_of(piece_ref[0, :, at], piece_ref[1, :, at], low, right, level_ref[:, at])
        share = jnp.where(live_mask(begin, end, base + start, cols), 1.0 - kept, 0.0)
        out_ref[0, :, at] = (real * share).astype(BF16)
        out_ref[1, :, at] = (imag * share).astype(BF16)

    for way, right_ref in zip(ways, right_refs):
        one(right_ref[...], device_at(-way[0], -way[1]))
    if not ways:
        block = column_block(right_refs[0].shape[0])

        @pl.loop(0, right_refs[0].shape[0] // block)
        def _(step):
            one(right_refs[0][pl.ds(pl.multiple_of(step * block, block), block), :], step)


def join_body(ways, header_ref, move_ref, rows_ref, mine_ref, *refs):
    narrow = lax.axis_size("narrow") - 1
    other_refs, refs = refs[:narrow], refs[narrow:]
    many = len(ways) or 1
    low_refs, change_refs, (out_ref, rows_out_ref) = refs[:many], refs[many : 2 * many], refs[2 * many :]
    for way, low_ref, change_ref in zip(ways, low_refs, change_refs):
        cols = low_ref.shape[0]
        at = pl.ds(pl.multiple_of(device_at(-way[0], -way[1]) * cols, cols), cols)
        out_ref[at, :] = low_ref[...].astype(F32) + change_ref[...].astype(F32)
    if not ways:
        out_ref[...] = low_refs[0][...].astype(F32) + change_refs[0][...].astype(F32)

    total = mine_ref[...]
    for other_ref in other_refs:
        total = total + other_ref[...]
    rows = total.shape[0] - PAD
    norm = both_halves(total[rows : rows + 1] + total[rows + 1 : rows + 2])
    my_row = lax.axis_index("wide") * rows + lax.broadcasted_iota(jnp.int32, (rows, rows), 0)
    first = jnp.zeros(rows_ref.shape, F32)
    for source in range(header_ref.shape[0]):
        named = header_ref[source, rows : rows + 1, :rows].astype(jnp.int32)
        place = jnp.where(my_row == named, 1.0, 0.0).astype(BF16)
        first = first + jnp.dot(place, move_ref[source], preferred_element_type=F32)
    rows_out_ref[...] = rows_ref[...] + first + total[:rows] / (norm + epsilon)


VMEM = pl.BlockSpec(memory_space=pltpu.VMEM)


def call(body, shapes, arrays, scratch=()):
    return pl.pallas_call(
        body,
        in_specs=[VMEM] * len(arrays),
        out_specs=jax.tree.map(lambda _: VMEM, shapes),
        out_shape=shapes,
        scratch_shapes=list(scratch),
    )(*arrays)


def column_block(count):
    block = min(512, count)
    while count % block:
        block //= 2
    return block


def exchange(blocks):
    return lax.all_to_all(blocks, "wide", split_axis=0, concat_axis=0, tiled=True)


def other_narrow(value):
    count = lax.axis_size("narrow")
    return [lax.ppermute(value, "narrow", [(i, (i + k) % count) for i in range(count)]) for k in range(1, count)]


def small_wide():
    count = lax.axis_size("wide")
    return count % NEAR == 0 and count <= 4 * NEAR


def shift(value, far, near):
    outer = lax.axis_size("wide") // NEAR
    pairs = [
        (z * NEAR + x, (z + far) % outer * NEAR + (x + near) % NEAR) for z in range(outer) for x in range(NEAR)
    ]
    return lax.ppermute(value, "wide", pairs)


def device_at(far, near):
    outer = lax.axis_size("wide") // NEAR
    me = lax.axis_index("wide")
    return (me // NEAR + far) % outer * NEAR + (me % NEAR + near) % NEAR


def part_ways():
    if not small_wide():
        return ()
    outer = lax.axis_size("wide") // NEAR
    far_first = sorted(range(1, outer), key=lambda far: -min(far, outer - far))
    ways = [(far, near) for far in far_first for near in range(NEAR)]
    return (*ways, *((0, near) for near in range(1, NEAR)), (0, 0))


def gather_ways():
    if not small_wide():
        return ()
    return tuple((far, near) for far in range(lax.axis_size("wide") // NEAR) for near in range(NEAR))


def gather_parts(block):
    count = lax.axis_size("wide")
    ways = gather_ways()
    if not ways:
        return [exchange(jnp.broadcast_to(block[None], (count,) + block.shape)).reshape(-1, block.shape[1])]
    held = {(far, 0): shift(block, far, 0) for far, near in ways if far and not near}
    held |= {(0, near): shift(block, 0, near) for near in range(1, NEAR)}
    held[0, 0] = block
    return [held[way] if way in held else shift(held[way[0], 0], 0, way[1]) for way in ways]


def program(pieces, destination, first_offset, valid_length, midpoint_factor, offset_factor, threshold):
    count = lax.axis_size("wide")
    _, rows, cols = pieces.shape
    width = offset_factor.shape[1]
    part = cols // count
    total = count * rows
    level = threshold[None, :]
    own_level = level
    if part % 128:
        own_level = lax.dynamic_slice_in_dim(level, lax.axis_index("wide") * part, part, 1)

    ways = part_ways()
    shape = jax.ShapeDtypeStruct
    header, numbers, *parts = call(
        partial(prep_body, ways),
        [shape((count, rows + PAD, width), F32), shape((PAD, width), F32)]
        + [shape((2, rows, part), pieces.dtype)] * len(ways),
        [midpoint_factor, destination[None], first_offset[None], valid_length[None]] + [pieces] * bool(ways),
    )
    headers = exchange(header)
    if ways:
        blocks = [block if way == (0, 0) else shift(block, *way) for way, block in zip(ways, parts)]
    else:
        blocks = [exchange(jnp.transpose(pieces.reshape(2, rows, count, part), (2, 0, 1, 3)))]

    row_grad, left_mine, own_right = call(
        rows_body,
        [shape((rows + PAD, width), F32), shape((rows, width), F32), shape((part, width), F32)],
        [pieces, headers, numbers, offset_factor, level],
        [pltpu.VMEM((2 * rows, width), F32), pltpu.VMEM((8, width), F32)],
    )
    move_mine, moves = call(
        step_body, [shape((rows, width), BF16), shape((count, rows, width), BF16)], [row_grad] + other_narrow(row_grad)
    )
    moves = exchange(moves)

    right_one, right_low, left_all = call(
        partial(cols_body, ways, False),
        [shape((part, width), F32), shape((part, width), BF16), shape((total, width), F32)],
        [headers, own_right, own_level, *blocks],
        [pltpu.VMEM((width, part), F32)],
    )
    lows = gather_parts(right_low)

    change, outgoing = call(
        partial(cols_body, ways, True),
        [shape((part, width), BF16), shape((count, rows + PAD, width), BF16)],
        [headers, right_one, own_level, *blocks, left_all, moves.reshape(total, width)],
        [pltpu.VMEM((width, part), F32), pltpu.VMEM((total, width), F32)],
    )
    changes = gather_parts(change)
    arrived = exchange(outgoing)
    summed = jnp.sum(arrived.astype(F32), 0)

    sparse = call(
        partial(sparse_body, gather_ways()),
        shape(pieces.shape, BF16),
        [pieces, numbers, left_mine, move_mine, level, *lows],
    )
    new_offset, new_midpoint = call(
        partial(join_body, gather_ways()),
        [shape((cols, width), F32), shape((rows, width), F32)],
        [headers, moves, midpoint_factor, summed, *other_narrow(summed), *lows, *changes],
    )
    return sparse, new_midpoint, new_offset


def solution(mesh):
    placed = (
        P(None, ("groups", "wide"), "narrow"),
        P("wide"),
        P("wide"),
        P("wide"),
        P(("groups", "wide"), None),
        P(("groups", "narrow"), None),
        P(("groups", "narrow")),
    )
    return jax.shard_map(
        program,
        mesh=mesh,
        in_specs=placed,
        out_specs=(
            P(None, ("groups", "wide"), "narrow"),
            P(("groups", "wide"), None),
            P(("groups", "narrow"), None),
        ),
        check_vma=False,
    )
```

```python
from functools import partial

import jax
import jax.numpy as jnp
from jax import lax
from jax.experimental import pallas as pl
from jax.experimental.pallas import tpu as pltpu
from jax.sharding import PartitionSpec as P


epsilon = 1e-06
F32 = jnp.float32
BF16 = jnp.bfloat16
PAD = 8
NEAR = 2


def turned(rows):
    half = rows.shape[1] // 2
    return jnp.concatenate([rows[:, half:], -rows[:, :half]], 1)


def unturned(rows):
    half = rows.shape[1] // 2
    return jnp.concatenate([-rows[:, half:], rows[:, :half]], 1)


def both_halves(norm):
    half = norm.shape[1] // 2
    once = norm[:, :half] + norm[:, half:]
    return jnp.concatenate([once, once], 1)


def pair_of(left_low):
    return jnp.concatenate([left_low, turned(left_low)], 0)


def model_of(pair, right_low):
    return lax.dot_general(pair, right_low, (((1,), (1,)), ((), ())), preferred_element_type=F32)


def residual_of(piece_real, piece_imag, model, level):
    rows = model.shape[0] // 2
    real = piece_real.astype(F32) - model[:rows]
    imag = piece_imag.astype(F32) - model[rows:]
    kept = level * lax.rsqrt(jnp.maximum(real * real + imag * imag, level * level))
    return real, imag, kept


def live_mask(begin, end, first_col, count):
    column = lax.broadcasted_iota(jnp.int32, (begin.shape[0], count), 1)
    return (column >= begin - first_col) & (column < end - first_col)


def masked_error(real, imag, kept, inside):
    share = jnp.where(inside, kept, 0.0)
    return jnp.concatenate([(real * share).astype(BF16), (imag * share).astype(BF16)], 0)


BASE = 128


def row_numbers(dest_ref, first_ref, valid_ref, rows_ref):
    first = first_ref[...]
    end = first + valid_ref[...]
    both = jnp.concatenate(
        [jnp.concatenate([dest_ref[...], first], 1), jnp.concatenate([end, jnp.zeros_like(end)], 1)], 0
    )
    high = both >> (BASE.bit_length() - 1)
    table = rows_ref[...]
    norm = [way.astype(F32) for way in three_ways(jnp.sum(table * table, 0, keepdims=True))]
    low = (both & (BASE - 1)).astype(F32)
    return jnp.concatenate([high.astype(F32), low, *norm, jnp.zeros((PAD - 7, table.shape[1]), F32)], 0).astype(BF16)


def read_numbers(numbers):
    value = numbers.astype(F32)
    return value[0:2] * BASE + value[2:4]


def standing_numbers(numbers, rows):
    value = read_numbers(numbers)
    value = jnp.concatenate([value, jnp.zeros((6, value.shape[1]), F32)], 0)
    columns = value.T.astype(jnp.int32)
    return columns[:rows, 0:1], columns[rows : 2 * rows, 0:1], columns[:rows, 1:2]


def three_ways(table):
    high = table.astype(BF16)
    rest = table - high.astype(F32)
    middle = rest.astype(BF16)
    return [high, middle, (rest - middle.astype(F32)).astype(BF16)]


def picked(dest, table):
    row = lax.broadcasted_iota(jnp.int32, (dest.shape[0], table.shape[0]), 1)
    place = jnp.where(row == dest, 1.0, 0.0).astype(BF16)
    return jnp.dot(place, table, preferred_element_type=F32).astype(BF16)


def prep_body(ways, rows_ref, dest_ref, first_ref, valid_ref, *refs):
    piece_ref, header_ref, numbers_ref, *part_refs = refs if ways else (None, *refs)
    count, tall, _ = header_ref.shape
    rows = tall - PAD
    numbers = row_numbers(dest_ref, first_ref, valid_ref, rows_ref)
    numbers_ref[...] = numbers
    low = rows_ref[...].astype(BF16)
    for target in range(count):
        header_ref[target, :rows] = low
        header_ref[target, rows:] = numbers
    for way, part_ref in zip(ways, part_refs):
        cols = part_ref.shape[2]
        part_ref[...] = piece_ref[:, :, pl.ds(pl.multiple_of(device_at(*way) * cols, cols), cols)]


def rows_body(piece_ref, header_ref, numbers_ref, right_ref, level_ref, *refs):
    grad_ref, left_ref, own_ref = refs
    rows, width = left_ref.shape
    cols = right_ref.shape[0]
    part = own_ref.shape[0]
    block = column_block(cols)
    base = lax.axis_index("narrow") * cols
    dest, begin, end = standing_numbers(numbers_ref[...], rows)
    low = picked(dest, header_ref[:, :rows].reshape(-1, width))
    left_ref[...] = low
    own_ref[...] = right_ref[pl.ds(pl.multiple_of(lax.axis_index("wide") * part, part), part), :]
    grad = jnp.zeros((2 * rows, width), F32)
    norm = jnp.zeros((8, width), F32)
    for start in range(0, cols, block):
        at = pl.ds(start, block)
        right = right_ref[at, :]
        right_low = right.astype(BF16)
        model = model_of(pair_of(low), right_low)
        real, imag, kept = residual_of(piece_ref[0, :, at], piece_ref[1, :, at], model, level_ref[:, at])
        error = masked_error(real, imag, kept, live_mask(begin, end, base + start, block))
        grad = grad + jnp.dot(error, right_low, preferred_element_type=F32)
        norm = norm + jnp.sum((right * right).reshape(-1, 8, width), 0)

    grad_ref[:rows] = grad[:rows] + unturned(grad[rows:])
    grad_ref[rows:] = jnp.broadcast_to(jnp.sum(norm, 0, keepdims=True), (PAD, width))


def step_body(mine_ref, *refs):
    *other_refs, move_ref, out_ref = refs
    total = mine_ref[...]
    for other_ref in other_refs:
        total = total + other_ref[...]
    rows = total.shape[0] - PAD
    move = (total[:rows] / (both_halves(total[rows : rows + 1]) + epsilon)).astype(BF16)
    move_ref[...] = move
    for target in range(out_ref.shape[0]):
        out_ref[target] = move


def cols_body(ways, second, header_ref, right_ref, level_ref, *refs):
    many = len(ways) or 1
    piece_refs, refs = refs[:many], refs[many:]
    if second:
        left_ref, move_ref, change_ref, out_ref, pair_ref, model_ref, error_ref, part_ref = refs
    else:
        next_ref, low_ref, left_ref, pair_ref, model_ref, error_ref = refs
    sources, tall, width = header_ref.shape
    rows = tall - PAD
    part = right_ref.shape[0]
    right = right_ref[...]
    right_low = right.astype(BF16)
    me = lax.axis_index("wide")
    base = lax.axis_index("narrow") * (sources * part) + me * part
    if level_ref.shape[1] == part:
        level = level_ref[...]
    else:
        level = level_ref[:, pl.ds(pl.multiple_of(me * part, part), part)]

    if second:
        left = left_ref[...].astype(F32) + move_ref[...].astype(F32)
        norm = jnp.sum(left * left, 0, keepdims=True)
        left_low = left.astype(BF16)
    else:
        norm = jnp.zeros((1, width), F32)
        for source in range(sources):
            norm = norm + jnp.sum(header_ref[source, rows:, :].astype(F32)[4:7], 0, keepdims=True)
        table = header_ref[:, :rows].reshape(-1, width)

    def place_pair(source, low):
        at = pl.ds(pl.multiple_of(source * 2 * rows, 2 * rows), 2 * rows)
        pair_ref[at, :] = pair_of(low)

    def pick(source):
        dest, _, _ = standing_numbers(header_ref[source, rows:, :], rows)
        low = picked(dest, table)
        left_ref[pl.ds(pl.multiple_of(source * rows, rows), rows), :] = low
        place_pair(source, low)

    def shrink(piece_real, piece_imag, source):
        at = pl.ds(pl.multiple_of(source * 2 * rows, 2 * rows), 2 * rows)
        _, begin, end = standing_numbers(header_ref[source, rows:, :], rows)
        real, imag, kept = residual_of(piece_real, piece_imag, model_ref[at, :], level)
        error_ref[at, :] = masked_error(real, imag, kept, live_mask(begin, end, base, part))

    if second:
        for source in range(sources):
            place_pair(source, left_low[source * rows : (source + 1) * rows])
    elif ways:
        for source in range(sources):
            pick(source)
    else:
        pl.loop(0, sources)(pick)

    model_ref[...] = model_of(pair_ref[...], right_low)
    for way, piece_ref in zip(ways, piece_refs):
        shrink(piece_ref[0], piece_ref[1], device_at(-way[0], -way[1]))
    if not ways:

        @pl.loop(0, sources)
        def _(source):
            shrink(piece_refs[0][source, 0], piece_refs[0][source, 1], source)

    grad = lax.dot_general(pair_ref[...], error_ref[...], (((0,), (0,)), ((), ())), preferred_element_type=F32)
    after = right + grad.T / (both_halves(norm) + epsilon)
    if not second:
        next_ref[...] = after
        low_ref[...] = after.astype(BF16)
        return
    change_ref[...] = (after - right_low.astype(F32)).astype(BF16)

    part_ref[...] = jnp.zeros_like(part_ref)

    def place_grads(source):
        at = pl.ds(pl.multiple_of(source * 2 * rows, 2 * rows), 2 * rows)
        grads = jnp.dot(error_ref[at, :], right_low, preferred_element_type=F32)
        grads = (grads[:rows] + unturned(grads[rows:])).astype(BF16)
        named = read_numbers(header_ref[source, rows:, :])[0:1, :rows].astype(jnp.int32)
        row = lax.broadcasted_iota(jnp.int32, (sources * rows, rows), 0)
        place = jnp.where(row == named, 1.0, 0.0).astype(BF16)
        part_ref[...] += jnp.dot(place, grads, preferred_element_type=F32)

    if ways:
        for source in range(sources):
            place_grads(source)
    else:
        pl.loop(0, sources)(place_grads)

    norm = jnp.sum(right * right, 0, keepdims=True)
    high = norm.astype(BF16).astype(F32)
    tail = jnp.concatenate([high, norm - high, jnp.zeros((PAD - 2, width), F32)], 0).astype(BF16)
    for target in range(sources):
        out_ref[target, :rows] = part_ref[target * rows : (target + 1) * rows].astype(BF16)
        out_ref[target, rows:] = tail


def sparse_body(ways, piece_ref, numbers_ref, left_ref, move_ref, level_ref, *refs):
    right_refs, out_ref = refs[:-1], refs[-1]
    low = (left_ref[...].astype(F32) + move_ref[...].astype(F32)).astype(BF16)
    _, begin, end = standing_numbers(numbers_ref[...], low.shape[0])
    base = lax.axis_index("narrow") * piece_ref.shape[2]

    def one(right, source):
        cols = right.shape[0]
        start = source * cols
        at = pl.ds(pl.multiple_of(start, cols), cols)
        model = model_of(pair_of(low), right)
        real, imag, kept = residual_of(piece_ref[0, :, at], piece_ref[1, :, at], model, level_ref[:, at])
        share = jnp.where(live_mask(begin, end, base + start, cols), 1.0 - kept, 0.0)
        out_ref[0, :, at] = (real * share).astype(BF16)
        out_ref[1, :, at] = (imag * share).astype(BF16)

    for way, right_ref in zip(ways, right_refs):
        one(right_ref[...], device_at(-way[0], -way[1]))
    if not ways:
        block = column_block(right_refs[0].shape[0])

        @pl.loop(0, right_refs[0].shape[0] // block)
        def _(step):
            one(right_refs[0][pl.ds(pl.multiple_of(step * block, block), block), :], step)


def join_body(ways, header_ref, move_ref, rows_ref, mine_ref, *refs):
    narrow = lax.axis_size("narrow") - 1
    other_refs, refs = refs[:narrow], refs[narrow:]
    many = len(ways) or 1
    low_refs, change_refs, refs = refs[:many], refs[many : 2 * many], refs[2 * many :]
    out_ref, rows_out_ref, held_ref, sem = refs
    copies = []
    for index, (low_ref, change_ref) in enumerate(zip(low_refs, change_refs)):
        cols = low_ref.shape[0]
        source = device_at(-ways[index][0], -ways[index][1]) if ways else 0
        held_ref[index] = low_ref[...].astype(F32) + change_ref[...].astype(F32)
        at = pl.ds(pl.multiple_of(source * cols, cols), cols)
        copies.append(pltpu.make_async_copy(held_ref.at[index], out_ref.at[at, :], sem.at[index]))
        copies[-1].start()

    total = mine_ref[...]
    for other_ref in other_refs:
        total = total + other_ref[...]
    rows = total.shape[0] - PAD
    norm = both_halves(total[rows : rows + 1] + total[rows + 1 : rows + 2])
    my_row = lax.axis_index("wide") * rows + lax.broadcasted_iota(jnp.int32, (rows, rows), 0)
    first = jnp.zeros(rows_ref.shape, F32)
    for source in range(header_ref.shape[0]):
        named = read_numbers(header_ref[source, rows:, :])[0:1, :rows].astype(jnp.int32)
        place = jnp.where(my_row == named, 1.0, 0.0).astype(BF16)
        first = first + jnp.dot(place, move_ref[source], preferred_element_type=F32)
    rows_out_ref[...] = rows_ref[...] + first + total[:rows] / (norm + epsilon)
    for copy in copies:
        copy.wait()


VMEM = pl.BlockSpec(memory_space=pltpu.VMEM)


ANY = pl.BlockSpec(memory_space=pl.ANY)


def call(body, shapes, arrays, scratch=(), out_specs=None):
    return pl.pallas_call(
        body,
        in_specs=[VMEM] * len(arrays),
        out_specs=out_specs or jax.tree.map(lambda _: VMEM, shapes),
        out_shape=shapes,
        scratch_shapes=list(scratch),
    )(*arrays)


def column_block(count):
    block = min(512, count)
    while count % block:
        block //= 2
    return block


def exchange(blocks):
    return lax.all_to_all(blocks, "wide", split_axis=0, concat_axis=0, tiled=True)


def other_narrow(value):
    count = lax.axis_size("narrow")
    return [lax.ppermute(value, "narrow", [(i, (i + k) % count) for i in range(count)]) for k in range(1, count)]


def small_wide():
    count = lax.axis_size("wide")
    return count % NEAR == 0 and count <= 4 * NEAR


def shift(value, far, near):
    outer = lax.axis_size("wide") // NEAR
    pairs = [
        (z * NEAR + x, (z + far) % outer * NEAR + (x + near) % NEAR) for z in range(outer) for x in range(NEAR)
    ]
    return lax.ppermute(value, "wide", pairs)


def device_at(far, near):
    outer = lax.axis_size("wide") // NEAR
    me = lax.axis_index("wide")
    return (me // NEAR + far) % outer * NEAR + (me % NEAR + near) % NEAR


def part_ways():
    if not small_wide():
        return ()
    outer = lax.axis_size("wide") // NEAR
    far_first = sorted(range(1, outer), key=lambda far: -min(far, outer - far))
    ways = [(far, near) for far in far_first for near in range(NEAR)]
    return (*ways, *((0, near) for near in range(1, NEAR)), (0, 0))


def gather_ways():
    if not small_wide():
        return ()
    return tuple((far, near) for far in range(lax.axis_size("wide") // NEAR) for near in range(NEAR))


def gather_parts(block, passed_on):
    count = lax.axis_size("wide")
    ways = gather_ways()
    if not ways:
        return [exchange(jnp.broadcast_to(block[None], (count,) + block.shape)).reshape(-1, block.shape[1])]
    outer = count // NEAR
    held = {(0, 0): block}
    for far in sorted(range(1, outer), key=lambda far: -min(far, outer - far)):
        held[far, 0] = shift(block, far, 0)
    for far in range(1, outer):
        if not passed_on(far, outer):
            held |= {(far, near): shift(block, far, near) for near in range(1, NEAR)}
    held |= {(0, near): shift(block, 0, near) for near in range(1, NEAR)}
    return [held[way] if way in held else shift(held[way[0], 0], 0, way[1]) for way in ways]


def program(pieces, destination, first_offset, valid_length, midpoint_factor, offset_factor, threshold):
    count = lax.axis_size("wide")
    _, rows, cols = pieces.shape
    width = offset_factor.shape[1]
    part = cols // count
    total = count * rows
    level = threshold[None, :]
    own_level = level
    if part % 128:
        own_level = lax.dynamic_slice_in_dim(level, lax.axis_index("wide") * part, part, 1)

    ways = part_ways()
    shape = jax.ShapeDtypeStruct
    header, numbers, *parts = call(
        partial(prep_body, ways),
        [shape((count, rows + PAD, width), BF16), shape((PAD, width), BF16)]
        + [shape((2, rows, part), pieces.dtype)] * len(ways),
        [midpoint_factor, destination[None], first_offset[None], valid_length[None]] + [pieces] * bool(ways),
    )
    headers = exchange(header)
    if ways:
        blocks = [block if way == (0, 0) else shift(block, *way) for way, block in zip(ways, parts)]
    else:
        blocks = [exchange(jnp.transpose(pieces.reshape(2, rows, count, part), (2, 0, 1, 3)))]

    row_grad, left_mine, own_right = call(
        rows_body,
        [shape((rows + PAD, width), F32), shape((rows, width), BF16), shape((part, width), F32)],
        [pieces, headers, numbers, offset_factor, level],
    )
    move_mine, moves = call(
        step_body, [shape((rows, width), BF16), shape((count, rows, width), BF16)], [row_grad] + other_narrow(row_grad)
    )
    moves = exchange(moves)

    held = [pltpu.VMEM((2 * total, width), BF16), pltpu.VMEM((2 * total, part), F32), pltpu.VMEM((2 * total, part), BF16)]
    right_one, right_low, left_all = call(
        partial(cols_body, ways, False),
        [shape((part, width), F32), shape((part, width), BF16), shape((total, width), BF16)],
        [headers, own_right, own_level, *blocks],
        held,
    )
    lows = gather_parts(right_low, passed_on=lambda far, outer: True)

    change, outgoing = call(
        partial(cols_body, ways, True),
        [shape((part, width), BF16), shape((count, rows + PAD, width), BF16)],
        [headers, right_one, own_level, *blocks, left_all, moves.reshape(total, width)],
        [*held, pltpu.VMEM((total, width), F32)],
    )
    changes = gather_parts(change, passed_on=lambda far, outer: 2 * far == outer and outer > 2)
    arrived = exchange(outgoing)
    summed = jnp.sum(arrived.astype(F32), 0)

    sparse = call(
        partial(sparse_body, gather_ways()),
        shape(pieces.shape, BF16),
        [pieces, numbers, left_mine, move_mine, level, *lows],
    )
    new_offset, new_midpoint = call(
        partial(join_body, gather_ways()),
        [shape((cols, width), F32), shape((rows, width), F32)],
        [headers, moves, midpoint_factor, summed, *other_narrow(summed), *lows, *changes],
        [pltpu.VMEM((len(lows), cols // len(lows), width), F32), pltpu.SemaphoreType.DMA((len(lows),))],
        [ANY, VMEM],
    )
    return sparse, new_midpoint, new_offset


def solution(mesh):
    placed = (
        P(None, ("groups", "wide"), "narrow"),
        P("wide"),
        P("wide"),
        P("wide"),
        P(("groups", "wide"), None),
        P(("groups", "narrow"), None),
        P(("groups", "narrow")),
    )
    return jax.shard_map(
        program,
        mesh=mesh,
        in_specs=placed,
        out_specs=(
            P(None, ("groups", "wide"), "narrow"),
            P(("groups", "wide"), None),
            P(("groups", "narrow"), None),
        ),
        check_vma=False,
    )
```

```python
import math
from functools import partial

import jax
import jax.numpy as jnp
from jax import lax
from jax.experimental import pallas as pl
from jax.experimental.pallas import tpu as pltpu
from jax.sharding import PartitionSpec as P


epsilon = 1e-06
F32 = jnp.float32
BF16 = jnp.bfloat16
PAD = 8
NEAR = 2


def turned(rows):
    half = rows.shape[1] // 2
    return jnp.concatenate([rows[:, half:], -rows[:, :half]], 1)


def unturned(rows):
    half = rows.shape[1] // 2
    return jnp.concatenate([-rows[:, half:], rows[:, :half]], 1)


def both_halves(norm):
    half = norm.shape[1] // 2
    once = norm[:, :half] + norm[:, half:]
    return jnp.concatenate([once, once], 1)


def pair_of(left_low):
    return jnp.concatenate([left_low, turned(left_low)], 0)


def model_of(pair, right_low):
    return lax.dot_general(pair, right_low, (((1,), (1,)), ((), ())), preferred_element_type=F32)


def residual_of(piece_real, piece_imag, model, level):
    rows = model.shape[0] // 2
    real = piece_real.astype(F32) - model[:rows]
    imag = piece_imag.astype(F32) - model[rows:]
    kept = level * lax.rsqrt(jnp.maximum(real * real + imag * imag, level * level))
    return real, imag, kept


def live_mask(begin, end, first_col, count):
    column = lax.broadcasted_iota(jnp.int32, (begin.shape[0], count), 1)
    return (column >= begin - first_col) & (column < end - first_col)


def masked_error(real, imag, kept, inside):
    share = jnp.where(inside, kept, 0.0)
    return jnp.concatenate([(real * share).astype(BF16), (imag * share).astype(BF16)], 0)


BASE = 128


def row_numbers(dest_ref, first_ref, valid_ref, rows_ref):
    first = first_ref[...]
    end = first + valid_ref[...]
    both = jnp.concatenate(
        [jnp.concatenate([dest_ref[...], first], 1), jnp.concatenate([end, jnp.zeros_like(end)], 1)], 0
    )
    high = both >> (BASE.bit_length() - 1)
    table = rows_ref[...]
    norm = [way.astype(F32) for way in three_ways(jnp.sum(table * table, 0, keepdims=True))]
    low = (both & (BASE - 1)).astype(F32)
    return jnp.concatenate([high.astype(F32), low, *norm, jnp.zeros((PAD - 7, table.shape[1]), F32)], 0).astype(BF16)


def read_numbers(numbers):
    value = numbers.astype(F32)
    return value[0:2] * BASE + value[2:4]


def standing_numbers(numbers, rows):
    value = read_numbers(numbers)
    value = jnp.concatenate([value, jnp.zeros((6, value.shape[1]), F32)], 0)
    columns = value.T.astype(jnp.int32)
    return columns[:rows, 0:1], columns[rows : 2 * rows, 0:1], columns[:rows, 1:2]


def three_ways(table):
    high = table.astype(BF16)
    rest = table - high.astype(F32)
    middle = rest.astype(BF16)
    return [high, middle, (rest - middle.astype(F32)).astype(BF16)]


def picked(dest, table):
    row = lax.broadcasted_iota(jnp.int32, (dest.shape[0], table.shape[0]), 1)
    place = jnp.where(row == dest, 1.0, 0.0).astype(BF16)
    return jnp.dot(place, table, preferred_element_type=F32).astype(BF16)


def prep_body(ways, rows_ref, dest_ref, first_ref, valid_ref, *refs):
    piece_ref, header_ref, numbers_ref, *part_refs = refs if ways else (None, *refs)
    count, tall, _ = header_ref.shape
    rows = tall - PAD
    numbers = row_numbers(dest_ref, first_ref, valid_ref, rows_ref)
    numbers_ref[...] = numbers
    low = rows_ref[...].astype(BF16)
    for target in range(count):
        header_ref[target, :rows] = low
        header_ref[target, rows:] = numbers
    for way, part_ref in zip(ways, part_refs):
        cols = part_ref.shape[2]
        part_ref[...] = piece_ref[:, :, pl.ds(pl.multiple_of(device_at(*way) * cols, cols), cols)]


def rows_body(piece_ref, header_ref, numbers_ref, right_ref, level_ref, *refs):
    grad_ref, left_ref, own_ref = refs
    rows, width = left_ref.shape
    cols = right_ref.shape[0]
    part = own_ref.shape[0]
    block = column_block(cols)
    base = lax.axis_index("narrow") * cols
    dest, begin, end = standing_numbers(numbers_ref[...], rows)
    low = picked(dest, header_ref[:, :rows].reshape(-1, width))
    left_ref[...] = low
    own_ref[...] = right_ref[pl.ds(pl.multiple_of(lax.axis_index("wide") * part, part), part), :]
    grad = jnp.zeros((2 * rows, width), F32)
    norm = jnp.zeros((8, width), F32)
    for start in range(0, cols, block):
        at = pl.ds(start, block)
        right = right_ref[at, :]
        right_low = right.astype(BF16)
        model = model_of(pair_of(low), right_low)
        real, imag, kept = residual_of(piece_ref[0, :, at], piece_ref[1, :, at], model, level_ref[:, at])
        error = masked_error(real, imag, kept, live_mask(begin, end, base + start, block))
        grad = grad + jnp.dot(error, right_low, preferred_element_type=F32)
        norm = norm + jnp.sum((right * right).reshape(-1, 8, width), 0)

    grad_ref[:rows] = grad[:rows] + unturned(grad[rows:])
    grad_ref[rows:] = jnp.broadcast_to(jnp.sum(norm, 0, keepdims=True), (PAD, width))


def step_body(mine_ref, *refs):
    *other_refs, move_ref, out_ref = refs
    total = mine_ref[...]
    for other_ref in other_refs:
        total = total + other_ref[...]
    rows = total.shape[0] - PAD
    move = (total[:rows] / (both_halves(total[rows : rows + 1]) + epsilon)).astype(BF16)
    move_ref[...] = move
    for target in range(out_ref.shape[0]):
        out_ref[target] = move


def cols_body(ways, second, header_ref, right_ref, level_ref, *refs):
    many = len(ways) or 1
    piece_refs, refs = refs[:many], refs[many:]
    if second:
        left_ref, move_ref, change_ref, out_ref, pair_ref, model_ref, error_ref, part_ref = refs
    else:
        next_ref, low_ref, left_ref, pair_ref, model_ref, error_ref = refs
    sources, tall, width = header_ref.shape
    rows = tall - PAD
    part = right_ref.shape[0]
    right = right_ref[...]
    right_low = right.astype(BF16)
    me = lax.axis_index("wide")
    base = lax.axis_index("narrow") * (sources * part) + me * part
    if level_ref.shape[1] == part:
        level = level_ref[...]
    else:
        level = level_ref[:, pl.ds(pl.multiple_of(me * part, part), part)]

    if second:
        left = left_ref[...].astype(F32) + move_ref[...].astype(F32)
        norm = jnp.sum(left * left, 0, keepdims=True)
        left_low = left.astype(BF16)
    else:
        norm = jnp.zeros((1, width), F32)
        for source in range(sources):
            norm = norm + jnp.sum(header_ref[source, rows:, :].astype(F32)[4:7], 0, keepdims=True)
        table = header_ref[:, :rows].reshape(-1, width)

    def place_pair(source, low):
        at = pl.ds(pl.multiple_of(source * 2 * rows, 2 * rows), 2 * rows)
        pair_ref[at, :] = pair_of(low)

    def pick(source):
        dest, _, _ = standing_numbers(header_ref[source, rows:, :], rows)
        low = picked(dest, table)
        left_ref[pl.ds(pl.multiple_of(source * rows, rows), rows), :] = low
        place_pair(source, low)

    def shrink(piece_real, piece_imag, source):
        at = pl.ds(pl.multiple_of(source * 2 * rows, 2 * rows), 2 * rows)
        _, begin, end = standing_numbers(header_ref[source, rows:, :], rows)
        real, imag, kept = residual_of(piece_real, piece_imag, model_ref[at, :], level)
        error_ref[at, :] = masked_error(real, imag, kept, live_mask(begin, end, base, part))

    if second:
        for source in range(sources):
            place_pair(source, left_low[source * rows : (source + 1) * rows])
    elif ways:
        for source in range(sources):
            pick(source)
    else:
        pl.loop(0, sources)(pick)

    model_ref[...] = model_of(pair_ref[...], right_low)
    for way, piece_ref in zip(ways, piece_refs):
        shrink(piece_ref[0], piece_ref[1], device_at(*way))
    if not ways:

        @pl.loop(0, sources)
        def _(source):
            shrink(piece_refs[0][source, 0], piece_refs[0][source, 1], source)

    grad = lax.dot_general(pair_ref[...], error_ref[...], (((0,), (0,)), ((), ())), preferred_element_type=F32)
    after = right + grad.T / (both_halves(norm) + epsilon)
    if not second:
        next_ref[...] = after
        low_ref[...] = after.astype(BF16)
        return
    change_ref[...] = (after - right_low.astype(F32)).astype(BF16)

    part_ref[...] = jnp.zeros_like(part_ref)

    def place_grads(source):
        at = pl.ds(pl.multiple_of(source * 2 * rows, 2 * rows), 2 * rows)
        grads = jnp.dot(error_ref[at, :], right_low, preferred_element_type=F32)
        grads = (grads[:rows] + unturned(grads[rows:])).astype(BF16)
        named = read_numbers(header_ref[source, rows:, :])[0:1, :rows].astype(jnp.int32)
        row = lax.broadcasted_iota(jnp.int32, (sources * rows, rows), 0)
        place = jnp.where(row == named, 1.0, 0.0).astype(BF16)
        part_ref[...] += jnp.dot(place, grads, preferred_element_type=F32)

    if ways:
        for source in range(sources):
            place_grads(source)
    else:
        pl.loop(0, sources)(place_grads)

    norm = jnp.sum(right * right, 0, keepdims=True)
    high = norm.astype(BF16).astype(F32)
    tail = jnp.concatenate([high, norm - high, jnp.zeros((PAD - 2, width), F32)], 0).astype(BF16)
    for target in range(sources):
        out_ref[target, :rows] = part_ref[target * rows : (target + 1) * rows].astype(BF16)
        out_ref[target, rows:] = tail


def sparse_body(ways, piece_ref, numbers_ref, left_ref, move_ref, level_ref, *refs):
    right_refs, out_ref = refs[:-1], refs[-1]
    low = (left_ref[...].astype(F32) + move_ref[...].astype(F32)).astype(BF16)
    _, begin, end = standing_numbers(numbers_ref[...], low.shape[0])
    base = lax.axis_index("narrow") * piece_ref.shape[2]

    def one(right, source):
        cols = right.shape[0]
        start = source * cols
        at = pl.ds(pl.multiple_of(start, cols), cols)
        model = model_of(pair_of(low), right)
        real, imag, kept = residual_of(piece_ref[0, :, at], piece_ref[1, :, at], model, level_ref[:, at])
        share = jnp.where(live_mask(begin, end, base + start, cols), 1.0 - kept, 0.0)
        out_ref[0, :, at] = (real * share).astype(BF16)
        out_ref[1, :, at] = (imag * share).astype(BF16)

    for way, right_ref in zip(ways, right_refs):
        one(right_ref[...], device_at(*way))
    if not ways:
        block = column_block(right_refs[0].shape[0])

        @pl.loop(0, right_refs[0].shape[0] // block)
        def _(step):
            one(right_refs[0][pl.ds(pl.multiple_of(step * block, block), block), :], step)


def join_body(ways, header_ref, move_ref, rows_ref, mine_ref, *refs):
    narrow = lax.axis_size("narrow") - 1
    other_refs, refs = refs[:narrow], refs[narrow:]
    many = len(ways) or 1
    low_refs, change_refs, refs = refs[:many], refs[many : 2 * many], refs[2 * many :]
    out_ref, rows_out_ref, held_ref, sem = refs
    copies = []
    for index, (low_ref, change_ref) in enumerate(zip(low_refs, change_refs)):
        cols = low_ref.shape[0]
        source = device_at(*ways[index]) if ways else 0
        held_ref[index] = low_ref[...].astype(F32) + change_ref[...].astype(F32)
        at = pl.ds(pl.multiple_of(source * cols, cols), cols)
        copies.append(pltpu.make_async_copy(held_ref.at[index], out_ref.at[at, :], sem.at[index]))
        copies[-1].start()

    total = mine_ref[...]
    for other_ref in other_refs:
        total = total + other_ref[...]
    rows = total.shape[0] - PAD
    norm = both_halves(total[rows : rows + 1] + total[rows + 1 : rows + 2])
    my_row = lax.axis_index("wide") * rows + lax.broadcasted_iota(jnp.int32, (rows, rows), 0)
    first = jnp.zeros(rows_ref.shape, F32)
    for source in range(header_ref.shape[0]):
        named = read_numbers(header_ref[source, rows:, :])[0:1, :rows].astype(jnp.int32)
        place = jnp.where(my_row == named, 1.0, 0.0).astype(BF16)
        first = first + jnp.dot(place, move_ref[source], preferred_element_type=F32)
    rows_out_ref[...] = rows_ref[...] + first + total[:rows] / (norm + epsilon)
    for copy in copies:
        copy.wait()


VMEM = pl.BlockSpec(memory_space=pltpu.VMEM)


SMALL = 400000


def small(value):
    return math.prod(value.shape) * jnp.dtype(value.dtype).itemsize < SMALL


ANY = pl.BlockSpec(memory_space=pl.ANY)


def call(body, name, shapes, arrays, scratch=(), out_specs=None, keep=True):
    if keep:
        shapes = jax.tree.map(lambda v: pltpu.VMEM(v.shape, v.dtype) if small(v) else v, shapes)
    if name != "prep":
        arrays = [pltpu.with_memory_space_constraint(v, pltpu.VMEM) if small(v) else v for v in arrays]
    return pl.pallas_call(
        body,
        in_specs=[VMEM] * len(arrays),
        out_specs=out_specs or jax.tree.map(lambda _: VMEM, shapes),
        out_shape=shapes,
        scratch_shapes=list(scratch),
    )(*arrays)


def column_block(count):
    block = min(512, count)
    while count % block:
        block //= 2
    return block


def exchange(blocks):
    return lax.all_to_all(blocks, "wide", split_axis=0, concat_axis=0, tiled=True)


def other_narrow(value):
    count = lax.axis_size("narrow")
    return [lax.ppermute(value, "narrow", [(i, (i + k) % count) for i in range(count)]) for k in range(1, count)]


def small_wide():
    count = lax.axis_size("wide")
    return count % NEAR == 0 and count <= 4 * NEAR


def shift(value, far, near):
    outer = lax.axis_size("wide") // NEAR
    pairs = [
        (z * NEAR + x, (z ^ far) * NEAR + (x ^ near)) for z in range(outer) for x in range(NEAR)
    ]
    return lax.ppermute(value, "wide", pairs)


def device_at(far, near):
    me = lax.axis_index("wide")
    return ((me // NEAR) ^ far) * NEAR + ((me % NEAR) ^ near)


def part_ways():
    if not small_wide():
        return ()
    outer = lax.axis_size("wide") // NEAR
    far_first = sorted(range(1, outer), key=lambda far: -min(far, outer - far))
    ways = [(far, near) for far in far_first for near in range(NEAR)]
    return (*((0, near) for near in range(1, NEAR)), *reversed(ways), (0, 0))


def gather_ways():
    if not small_wide():
        return ()
    return tuple((far, near) for far in range(lax.axis_size("wide") // NEAR) for near in range(NEAR))


def gather_parts(block, passed_on):
    count = lax.axis_size("wide")
    ways = gather_ways()
    if not ways:
        return [exchange(jnp.broadcast_to(block[None], (count,) + block.shape)).reshape(-1, block.shape[1])]
    outer = count // NEAR
    held = {(0, 0): block}
    for far in sorted(range(1, outer), key=lambda far: -min(far, outer - far)):
        held[far, 0] = shift(block, far, 0)
    for far in range(1, outer):
        if not passed_on(far, outer):
            held |= {(far, near): shift(block, far, near) for near in range(1, NEAR)}
    held |= {(0, near): shift(block, 0, near) for near in range(1, NEAR)}
    return [held[way] if way in held else shift(held[way[0], 0], 0, way[1]) for way in ways]


def program(pieces, destination, first_offset, valid_length, midpoint_factor, offset_factor, threshold):
    count = lax.axis_size("wide")
    _, rows, cols = pieces.shape
    width = offset_factor.shape[1]
    part = cols // count
    total = count * rows
    level = threshold[None, :]
    own_level = level
    if part % 128:
        own_level = lax.dynamic_slice_in_dim(level, lax.axis_index("wide") * part, part, 1)

    ways = part_ways()
    shape = jax.ShapeDtypeStruct
    header, numbers, *parts = call(
        partial(prep_body, ways),
        "prep",
        [shape((count, rows + PAD, width), BF16), shape((PAD, width), BF16)]
        + [shape((2, rows, part), pieces.dtype)] * len(ways),
        [midpoint_factor, destination[None], first_offset[None], valid_length[None]] + [pieces] * bool(ways),
        keep=False,
    )
    headers = exchange(header)
    if ways:
        blocks = [block if way == (0, 0) else shift(block, *way) for way, block in zip(ways, parts)]
    else:
        blocks = [exchange(jnp.transpose(pieces.reshape(2, rows, count, part), (2, 0, 1, 3)))]

    row_grad, left_mine, own_right = call(
        rows_body,
        "row_pass",
        [shape((rows + PAD, width), F32), shape((rows, width), BF16), shape((part, width), F32)],
        [pieces, headers, numbers, offset_factor, level],
    )
    move_mine, moves = call(
        step_body,
        "step",
        [shape((rows, width), BF16), shape((count, rows, width), BF16)],
        [row_grad] + other_narrow(row_grad),
    )
    moves = exchange(moves)

    held = [pltpu.VMEM((2 * total, width), BF16), pltpu.VMEM((2 * total, part), F32), pltpu.VMEM((2 * total, part), BF16)]
    right_one, right_low, left_all = call(
        partial(cols_body, ways, False),
        "col_pass_1",
        [shape((part, width), F32), shape((part, width), BF16), shape((total, width), BF16)],
        [headers, own_right, own_level, *blocks],
        held,
    )
    lows = gather_parts(right_low, passed_on=lambda far, outer: True)

    change, outgoing = call(
        partial(cols_body, ways, True),
        "col_pass_2",
        [shape((part, width), BF16), shape((count, rows + PAD, width), BF16)],
        [headers, right_one, own_level, *blocks, left_all, moves.reshape(total, width)],
        [*held, pltpu.VMEM((total, width), F32)],
    )
    changes = gather_parts(change, passed_on=lambda far, outer: True)
    arrived = exchange(outgoing)
    summed = jnp.sum(arrived.astype(F32), 0)

    sparse = call(
        partial(sparse_body, gather_ways()),
        "sparse_pass",
        shape(pieces.shape, BF16),
        [pieces, numbers, left_mine, move_mine, level, *lows],
        keep=False,
    )
    new_offset, new_midpoint = call(
        partial(join_body, gather_ways()),
        "join",
        [shape((cols, width), F32), shape((rows, width), F32)],
        [headers, moves, midpoint_factor, summed, *other_narrow(summed), *lows, *changes],
        [pltpu.VMEM((len(lows), cols // len(lows), width), F32), pltpu.SemaphoreType.DMA((len(lows),))],
        [ANY, VMEM],
        keep=False,
    )
    return sparse, new_midpoint, new_offset


def solution(mesh):
    placed = (
        P(None, ("groups", "wide"), "narrow"),
        P("wide"),
        P("wide"),
        P("wide"),
        P(("groups", "wide"), None),
        P(("groups", "narrow"), None),
        P(("groups", "narrow")),
    )
    return jax.shard_map(
        program,
        mesh=mesh,
        in_specs=placed,
        out_specs=(
            P(None, ("groups", "wide"), "narrow"),
            P(("groups", "wide"), None),
            P(("groups", "narrow"), None),
        ),
        check_vma=False,
    )
```

```python
import math
from functools import partial

import jax
import jax.numpy as jnp
from jax import lax
from jax.experimental import pallas as pl
from jax.experimental.pallas import tpu as pltpu
from jax.sharding import PartitionSpec as P


epsilon = 1e-06
F32 = jnp.float32
BF16 = jnp.bfloat16
PAD = 8
NEAR = 2


def turned(rows):
    half = rows.shape[1] // 2
    return jnp.concatenate([rows[:, half:], -rows[:, :half]], 1)


def unturned(rows):
    half = rows.shape[1] // 2
    return jnp.concatenate([-rows[:, half:], rows[:, :half]], 1)


def both_halves(norm):
    half = norm.shape[1] // 2
    once = norm[:, :half] + norm[:, half:]
    return jnp.concatenate([once, once], 1)


def pair_of(left_low):
    return jnp.concatenate([left_low, turned(left_low)], 0)


def model_of(pair, right_low):
    return lax.dot_general(pair, right_low, (((1,), (1,)), ((), ())), preferred_element_type=F32)


def residual_of(piece_real, piece_imag, model, level):
    rows = model.shape[0] // 2
    real = piece_real.astype(F32) - model[:rows]
    imag = piece_imag.astype(F32) - model[rows:]
    kept = level * lax.rsqrt(jnp.maximum(real * real + imag * imag, level * level))
    return real, imag, kept


def live_mask(begin, end, first_col, count):
    column = lax.broadcasted_iota(jnp.int32, (begin.shape[0], count), 1)
    return (column >= begin - first_col) & (column < end - first_col)


def masked_error(real, imag, kept, inside):
    share = jnp.where(inside, kept, 0.0)
    return jnp.concatenate([(real * share).astype(BF16), (imag * share).astype(BF16)], 0)


BASE = 128


def row_numbers(dest_ref, first_ref, valid_ref, rows_ref):
    first = first_ref[...]
    end = first + valid_ref[...]
    both = jnp.concatenate(
        [jnp.concatenate([dest_ref[...], first], 1), jnp.concatenate([end, jnp.zeros_like(end)], 1)], 0
    )
    high = both >> (BASE.bit_length() - 1)
    table = rows_ref[...]
    norm = [way.astype(F32) for way in three_ways(jnp.sum(table * table, 0, keepdims=True))]
    low = (both & (BASE - 1)).astype(F32)
    return jnp.concatenate([high.astype(F32), low, *norm, jnp.zeros((PAD - 7, table.shape[1]), F32)], 0).astype(BF16)


def read_numbers(numbers):
    value = numbers.astype(F32)
    return value[0:2] * BASE + value[2:4]


def standing_numbers(numbers, rows):
    value = read_numbers(numbers)
    value = jnp.concatenate([value, jnp.zeros((6, value.shape[1]), F32)], 0)
    columns = value.T.astype(jnp.int32)
    return columns[:rows, 0:1], columns[rows : 2 * rows, 0:1], columns[:rows, 1:2]


def three_ways(table):
    high = table.astype(BF16)
    rest = table - high.astype(F32)
    middle = rest.astype(BF16)
    return [high, middle, (rest - middle.astype(F32)).astype(BF16)]


def picked(dest, table):
    row = lax.broadcasted_iota(jnp.int32, (dest.shape[0], table.shape[0]), 1)
    place = jnp.where(row == dest, 1.0, 0.0).astype(BF16)
    return jnp.dot(place, table, preferred_element_type=F32).astype(BF16)


def prep_body(ways, rows_ref, dest_ref, first_ref, valid_ref, *refs):
    piece_ref, header_ref, numbers_ref, *part_refs = refs if ways else (None, *refs)
    count, tall, _ = header_ref.shape
    rows = tall - PAD
    numbers = row_numbers(dest_ref, first_ref, valid_ref, rows_ref)
    numbers_ref[...] = numbers
    low = rows_ref[...].astype(BF16)
    for target in range(count):
        header_ref[target, :rows] = low
        header_ref[target, rows:] = numbers
    for way, part_ref in zip(ways, part_refs):
        cols = part_ref.shape[2]
        part_ref[...] = piece_ref[:, :, pl.ds(pl.multiple_of(device_at(*way) * cols, cols), cols)]


def rows_body(piece_ref, header_ref, numbers_ref, right_ref, level_ref, *refs):
    grad_ref, left_ref, own_ref = refs
    rows, width = left_ref.shape
    cols = right_ref.shape[0]
    part = own_ref.shape[0]
    block = column_block(cols)
    base = lax.axis_index("narrow") * cols
    dest, begin, end = standing_numbers(numbers_ref[...], rows)
    low = picked(dest, header_ref[:, :rows].reshape(-1, width))
    left_ref[...] = low
    own_ref[...] = right_ref[pl.ds(pl.multiple_of(lax.axis_index("wide") * part, part), part), :]
    grad = jnp.zeros((2 * rows, width), F32)
    norm = jnp.zeros((8, width), F32)
    for start in range(0, cols, block):
        at = pl.ds(start, block)
        right = right_ref[at, :]
        right_low = right.astype(BF16)
        model = model_of(pair_of(low), right_low)
        real, imag, kept = residual_of(piece_ref[0, :, at], piece_ref[1, :, at], model, level_ref[:, at])
        error = masked_error(real, imag, kept, live_mask(begin, end, base + start, block))
        grad = grad + jnp.dot(error, right_low, preferred_element_type=F32)
        norm = norm + jnp.sum((right * right).reshape(-1, 8, width), 0)

    grad_ref[:rows] = grad[:rows] + unturned(grad[rows:])
    grad_ref[rows:] = jnp.broadcast_to(jnp.sum(norm, 0, keepdims=True), (PAD, width))


def step_body(mine_ref, *refs):
    *other_refs, move_ref, out_ref = refs
    total = mine_ref[...]
    for other_ref in other_refs:
        total = total + other_ref[...]
    rows = total.shape[0] - PAD
    move = (total[:rows] / (both_halves(total[rows : rows + 1]) + epsilon)).astype(BF16)
    move_ref[...] = move
    for target in range(out_ref.shape[0]):
        out_ref[target] = move


def cols_body(ways, second, header_ref, right_ref, level_ref, *refs):
    many = len(ways) or 1
    piece_refs, refs = refs[:many], refs[many:]
    if second:
        left_ref, move_ref, change_ref, out_ref, pair_ref, model_ref, error_ref, part_ref = refs
    else:
        next_ref, low_ref, left_ref, pair_ref, model_ref, error_ref = refs
    sources, tall, width = header_ref.shape
    rows = tall - PAD
    part = right_ref.shape[0]
    right = right_ref[...]
    right_low = right.astype(BF16)
    me = lax.axis_index("wide")
    base = lax.axis_index("narrow") * (sources * part) + me * part
    if level_ref.shape[1] == part:
        level = level_ref[...]
    else:
        level = level_ref[:, pl.ds(pl.multiple_of(me * part, part), part)]

    if second:
        left = left_ref[...].astype(F32) + move_ref[...].astype(F32)
        norm = jnp.sum(left * left, 0, keepdims=True)
        left_low = left.astype(BF16)
    else:
        norm = jnp.zeros((1, width), F32)
        for source in range(sources):
            norm = norm + jnp.sum(header_ref[source, rows:, :].astype(F32)[4:7], 0, keepdims=True)
        table = header_ref[:, :rows].reshape(-1, width)

    def place_pair(source, low):
        at = pl.ds(pl.multiple_of(source * 2 * rows, 2 * rows), 2 * rows)
        pair_ref[at, :] = pair_of(low)

    def pick(source):
        dest, _, _ = standing_numbers(header_ref[source, rows:, :], rows)
        low = picked(dest, table)
        left_ref[pl.ds(pl.multiple_of(source * rows, rows), rows), :] = low
        place_pair(source, low)

    def shrink(piece_real, piece_imag, source):
        at = pl.ds(pl.multiple_of(source * 2 * rows, 2 * rows), 2 * rows)
        _, begin, end = standing_numbers(header_ref[source, rows:, :], rows)
        real, imag, kept = residual_of(piece_real, piece_imag, model_ref[at, :], level)
        error_ref[at, :] = masked_error(real, imag, kept, live_mask(begin, end, base, part))

    if second:
        for source in range(sources):
            place_pair(source, left_low[source * rows : (source + 1) * rows])
    elif ways:
        for source in range(sources):
            pick(source)
    else:
        pl.loop(0, sources)(pick)

    model_ref[...] = model_of(pair_ref[...], right_low)
    for way, piece_ref in zip(ways, piece_refs):
        shrink(piece_ref[0], piece_ref[1], device_at(*way))
    if not ways:

        @pl.loop(0, sources)
        def _(source):
            shrink(piece_refs[0][source, 0], piece_refs[0][source, 1], source)

    grad = lax.dot_general(pair_ref[...], error_ref[...], (((0,), (0,)), ((), ())), preferred_element_type=F32)
    after = right + grad.T / (both_halves(norm) + epsilon)
    if not second:
        next_ref[...] = after
        low_ref[...] = after.astype(BF16)
        return
    change_ref[...] = (after - right_low.astype(F32)).astype(BF16)

    part_ref[...] = jnp.zeros_like(part_ref)

    def place_grads(source):
        at = pl.ds(pl.multiple_of(source * 2 * rows, 2 * rows), 2 * rows)
        grads = jnp.dot(error_ref[at, :], right_low, preferred_element_type=F32)
        grads = (grads[:rows] + unturned(grads[rows:])).astype(BF16)
        named = read_numbers(header_ref[source, rows:, :])[0:1, :rows].astype(jnp.int32)
        row = lax.broadcasted_iota(jnp.int32, (sources * rows, rows), 0)
        place = jnp.where(row == named, 1.0, 0.0).astype(BF16)
        part_ref[...] += jnp.dot(place, grads, preferred_element_type=F32)

    if ways:
        for source in range(sources):
            place_grads(source)
    else:
        pl.loop(0, sources)(place_grads)

    norm = jnp.sum(right * right, 0, keepdims=True)
    high = norm.astype(BF16).astype(F32)
    tail = jnp.concatenate([high, norm - high, jnp.zeros((PAD - 2, width), F32)], 0).astype(BF16)
    for target in range(sources):
        out_ref[target, :rows] = part_ref[target * rows : (target + 1) * rows].astype(BF16)
        out_ref[target, rows:] = tail


def sparse_body(ways, piece_ref, numbers_ref, left_ref, move_ref, level_ref, *refs):
    right_refs, out_ref = refs[:-1], refs[-1]
    low = (left_ref[...].astype(F32) + move_ref[...].astype(F32)).astype(BF16)
    _, begin, end = standing_numbers(numbers_ref[...], low.shape[0])
    base = lax.axis_index("narrow") * piece_ref.shape[2]

    def one(right, source):
        cols = right.shape[0]
        start = source * cols
        at = pl.ds(pl.multiple_of(start, cols), cols)
        model = model_of(pair_of(low), right)
        real, imag, kept = residual_of(piece_ref[0, :, at], piece_ref[1, :, at], model, level_ref[:, at])
        share = jnp.where(live_mask(begin, end, base + start, cols), 1.0 - kept, 0.0)
        out_ref[0, :, at] = (real * share).astype(BF16)
        out_ref[1, :, at] = (imag * share).astype(BF16)

    for way, right_ref in zip(ways, right_refs):
        one(right_ref[...], device_at(*way))
    if not ways:
        block = column_block(right_refs[0].shape[0])

        @pl.loop(0, right_refs[0].shape[0] // block)
        def _(step):
            one(right_refs[0][pl.ds(pl.multiple_of(step * block, block), block), :], step)


def join_body(ways, header_ref, move_ref, rows_ref, mine_ref, *refs):
    narrow = lax.axis_size("narrow") - 1
    other_refs, refs = refs[:narrow], refs[narrow:]
    many = len(ways) or 1
    low_refs, change_refs, refs = refs[:many], refs[many : 2 * many], refs[2 * many :]
    out_ref, rows_out_ref, held_ref, sem = refs
    copies = []
    for index, (low_ref, change_ref) in enumerate(zip(low_refs, change_refs)):
        cols = low_ref.shape[0]
        source = device_at(*ways[index]) if ways else 0
        held_ref[index] = low_ref[...].astype(F32) + change_ref[...].astype(F32)
        at = pl.ds(pl.multiple_of(source * cols, cols), cols)
        copies.append(pltpu.make_async_copy(held_ref.at[index], out_ref.at[at, :], sem.at[index]))
        copies[-1].start()

    total = mine_ref[...]
    for other_ref in other_refs:
        total = total + other_ref[...]
    rows = total.shape[0] - PAD
    norm = both_halves(total[rows : rows + 1] + total[rows + 1 : rows + 2])
    my_row = lax.axis_index("wide") * rows + lax.broadcasted_iota(jnp.int32, (rows, rows), 0)
    first = jnp.zeros(rows_ref.shape, F32)
    for source in range(header_ref.shape[0]):
        named = read_numbers(header_ref[source, rows:, :])[0:1, :rows].astype(jnp.int32)
        place = jnp.where(my_row == named, 1.0, 0.0).astype(BF16)
        first = first + jnp.dot(place, move_ref[source], preferred_element_type=F32)
    rows_out_ref[...] = rows_ref[...] + first + total[:rows] / (norm + epsilon)
    for copy in copies:
        copy.wait()


VMEM = pl.BlockSpec(memory_space=pltpu.VMEM)


SMALL = 400000


def small(value):
    return math.prod(value.shape) * jnp.dtype(value.dtype).itemsize < SMALL


ANY = pl.BlockSpec(memory_space=pl.ANY)


def call(body, name, shapes, arrays, scratch=(), out_specs=None, keep=True):
    if keep:
        shapes = jax.tree.map(lambda v: pltpu.VMEM(v.shape, v.dtype) if small(v) else v, shapes)
    if name != "prep":
        arrays = [pltpu.with_memory_space_constraint(v, pltpu.VMEM) if small(v) else v for v in arrays]
    return pl.pallas_call(
        body,
        in_specs=[VMEM] * len(arrays),
        out_specs=out_specs or jax.tree.map(lambda _: VMEM, shapes),
        out_shape=shapes,
        scratch_shapes=list(scratch),
    )(*arrays)


def column_block(count):
    block = min(512, count)
    while count % block:
        block //= 2
    return block


def exchange(blocks):
    return lax.all_to_all(blocks, "wide", split_axis=0, concat_axis=0, tiled=True)


def other_narrow(value):
    count = lax.axis_size("narrow")
    return [lax.ppermute(value, "narrow", [(i, (i + k) % count) for i in range(count)]) for k in range(1, count)]


def small_wide():
    return lax.axis_size("wide") in (NEAR, 2 * NEAR, 4 * NEAR)


def shift(value, far, near):
    outer = lax.axis_size("wide") // NEAR
    pairs = [
        (z * NEAR + x, (z ^ far) * NEAR + (x ^ near)) for z in range(outer) for x in range(NEAR)
    ]
    return lax.ppermute(value, "wide", pairs)


def device_at(far, near):
    me = lax.axis_index("wide")
    return ((me // NEAR) ^ far) * NEAR + ((me % NEAR) ^ near)


def part_ways():
    if not small_wide():
        return ()
    outer = lax.axis_size("wide") // NEAR
    far_first = sorted(range(1, outer), key=lambda far: -min(far, outer - far))
    ways = [(far, near) for far in far_first for near in range(NEAR)]
    return (*((0, near) for near in range(1, NEAR)), *reversed(ways), (0, 0))


def gather_ways():
    if not small_wide():
        return ()
    return tuple((far, near) for far in range(lax.axis_size("wide") // NEAR) for near in range(NEAR))


def gather_parts(block):
    count = lax.axis_size("wide")
    ways = gather_ways()
    if not ways:
        return [exchange(jnp.broadcast_to(block[None], (count,) + block.shape)).reshape(-1, block.shape[1])]
    outer = count // NEAR
    held = {(0, 0): block}
    far = 1
    while far < outer:
        held[far, 0] = shift(block, far, 0)
        far *= 2
    held[0, 1] = shift(block, 0, 1)
    if outer == 4:
        held[3, 0] = shift(held[2, 0], 1, 0)
    for way in ways:
        if way not in held and way[0] < 3:
            held[way] = shift(held[way[0], 0], 0, way[1])
    for way in ways:
        if way not in held:
            held[way] = shift(held[2, 1], 1, 0)
    return [held[way] for way in ways]


def program(pieces, destination, first_offset, valid_length, midpoint_factor, offset_factor, threshold):
    count = lax.axis_size("wide")
    _, rows, cols = pieces.shape
    width = offset_factor.shape[1]
    part = cols // count
    total = count * rows
    level = threshold[None, :]
    own_level = level
    if part % 128:
        own_level = lax.dynamic_slice_in_dim(level, lax.axis_index("wide") * part, part, 1)

    ways = part_ways()
    shape = jax.ShapeDtypeStruct
    header, numbers, *parts = call(
        partial(prep_body, ways),
        "prep",
        [shape((count, rows + PAD, width), BF16), shape((PAD, width), BF16)]
        + [shape((2, rows, part), pieces.dtype)] * len(ways),
        [midpoint_factor, destination[None], first_offset[None], valid_length[None]] + [pieces] * bool(ways),
        keep=False,
    )
    headers = exchange(header)
    if ways:
        blocks = []
        for way, block in zip(ways, parts):
            blocks.append(block if way == (0, 0) else shift(block, *way))
    else:
        blocks = [exchange(jnp.transpose(pieces.reshape(2, rows, count, part), (2, 0, 1, 3)))]

    row_grad, left_mine, own_right = call(
        rows_body,
        "row_pass",
        [shape((rows + PAD, width), F32), shape((rows, width), BF16), shape((part, width), F32)],
        [pieces, headers, numbers, offset_factor, level],
    )
    move_mine, moves = call(
        step_body,
        "step",
        [shape((rows, width), BF16), shape((count, rows, width), BF16)],
        [row_grad] + other_narrow(row_grad),
    )
    moves = exchange(moves)

    held = [pltpu.VMEM((2 * total, width), BF16), pltpu.VMEM((2 * total, part), F32), pltpu.VMEM((2 * total, part), BF16)]
    right_one, right_low, left_all = call(
        partial(cols_body, ways, False),
        "col_pass_1",
        [shape((part, width), F32), shape((part, width), BF16), shape((total, width), BF16)],
        [headers, own_right, own_level, *blocks],
        held,
    )
    lows = gather_parts(right_low)

    change, outgoing = call(
        partial(cols_body, ways, True),
        "col_pass_2",
        [shape((part, width), BF16), shape((count, rows + PAD, width), BF16)],
        [headers, right_one, own_level, *blocks, left_all, moves.reshape(total, width)],
        [*held, pltpu.VMEM((total, width), F32)],
    )
    changes = gather_parts(change)
    arrived = exchange(outgoing)
    summed = jnp.sum(arrived.astype(F32), 0)

    sparse = call(
        partial(sparse_body, gather_ways()),
        "sparse_pass",
        shape(pieces.shape, BF16),
        [pieces, numbers, left_mine, move_mine, level, *lows],
        keep=False,
    )
    new_offset, new_midpoint = call(
        partial(join_body, gather_ways()),
        "join",
        [shape((cols, width), F32), shape((rows, width), F32)],
        [headers, moves, midpoint_factor, summed, *other_narrow(summed), *lows, *changes],
        [pltpu.VMEM((len(lows), cols // len(lows), width), F32), pltpu.SemaphoreType.DMA((len(lows),))],
        [ANY, VMEM],
        keep=False,
    )
    return sparse, new_midpoint, new_offset


def solution(mesh):
    placed = (
        P(None, ("groups", "wide"), "narrow"),
        P("wide"),
        P("wide"),
        P("wide"),
        P(("groups", "wide"), None),
        P(("groups", "narrow"), None),
        P(("groups", "narrow")),
    )
    return jax.shard_map(
        program,
        mesh=mesh,
        in_specs=placed,
        out_specs=(
            P(None, ("groups", "wide"), "narrow"),
            P(("groups", "wide"), None),
            P(("groups", "narrow"), None),
        ),
        check_vma=False,
    )
```

```python
import math
from functools import partial

import jax
import jax.numpy as jnp
from jax import lax
from jax.experimental import pallas as pl
from jax.experimental.pallas import tpu as pltpu
from jax.sharding import PartitionSpec as P


epsilon = 1e-06
F32 = jnp.float32
BF16 = jnp.bfloat16
PAD = 8
NEAR = 2


def turned(rows):
    half = rows.shape[1] // 2
    return jnp.concatenate([rows[:, half:], -rows[:, :half]], 1)


def unturned(rows):
    half = rows.shape[1] // 2
    return jnp.concatenate([-rows[:, half:], rows[:, :half]], 1)


def both_halves(norm):
    half = norm.shape[1] // 2
    once = norm[:, :half] + norm[:, half:]
    return jnp.concatenate([once, once], 1)


def pair_of(left_low):
    return jnp.concatenate([left_low, turned(left_low)], 0)


def model_of(pair, right_low):
    return lax.dot_general(pair, right_low, (((1,), (1,)), ((), ())), preferred_element_type=F32)


def residual_of(piece_real, piece_imag, model, level):
    rows = model.shape[0] // 2
    real = piece_real.astype(F32) - model[:rows]
    imag = piece_imag.astype(F32) - model[rows:]
    kept = level * lax.rsqrt(jnp.maximum(real * real + imag * imag, level * level))
    return real, imag, kept


def live_mask(begin, end, first_col, count):
    column = lax.broadcasted_iota(jnp.int32, (begin.shape[0], count), 1)
    return (column >= begin - first_col) & (column < end - first_col)


def masked_error(real, imag, kept, inside):
    share = jnp.where(inside, kept, 0.0)
    return jnp.concatenate([(real * share).astype(BF16), (imag * share).astype(BF16)], 0)


BASE = 128


def row_numbers(dest_ref, first_ref, valid_ref, rows_ref):
    first = first_ref[...]
    end = first + valid_ref[...]
    both = jnp.concatenate(
        [jnp.concatenate([dest_ref[...], first], 1), jnp.concatenate([end, jnp.zeros_like(end)], 1)], 0
    )
    high = both >> (BASE.bit_length() - 1)
    table = rows_ref[...]
    norm = [way.astype(F32) for way in three_ways(jnp.sum(table * table, 0, keepdims=True))]
    low = (both & (BASE - 1)).astype(F32)
    return jnp.concatenate([high.astype(F32), low, *norm, jnp.zeros((PAD - 7, table.shape[1]), F32)], 0).astype(BF16)


def read_numbers(numbers):
    value = numbers.astype(F32)
    return value[0:2] * BASE + value[2:4]


def standing_numbers(numbers, rows):
    value = read_numbers(numbers)
    value = jnp.concatenate([value, jnp.zeros((6, value.shape[1]), F32)], 0)
    columns = value.T.astype(jnp.int32)
    return columns[:rows, 0:1], columns[rows : 2 * rows, 0:1], columns[:rows, 1:2]


def three_ways(table):
    high = table.astype(BF16)
    rest = table - high.astype(F32)
    middle = rest.astype(BF16)
    return [high, middle, (rest - middle.astype(F32)).astype(BF16)]


def picked(dest, table):
    row = lax.broadcasted_iota(jnp.int32, (dest.shape[0], table.shape[0]), 1)
    place = jnp.where(row == dest, 1.0, 0.0).astype(BF16)
    return jnp.dot(place, table, preferred_element_type=F32).astype(BF16)


def prep_body(ways, rows_ref, dest_ref, first_ref, valid_ref, *refs):
    level_in_ref, *refs = refs
    piece_ref, header_ref, numbers_ref, level_ref, *part_refs = refs if ways else (None, *refs)
    level_ref[...] = level_in_ref[...]
    count, tall, _ = header_ref.shape
    rows = tall - PAD
    numbers = row_numbers(dest_ref, first_ref, valid_ref, rows_ref)
    numbers_ref[...] = numbers
    low = rows_ref[...].astype(BF16)
    for target in range(count):
        header_ref[target, :rows] = low
        header_ref[target, rows:] = numbers
    for way, part_ref in zip(ways, part_refs):
        cols = part_ref.shape[2]
        part_ref[...] = piece_ref[:, :, pl.ds(pl.multiple_of(device_at(*way) * cols, cols), cols)]


def rows_body(piece_ref, header_ref, numbers_ref, right_ref, level_ref, *refs):
    grad_ref, left_ref, own_ref = refs
    rows, width = left_ref.shape
    cols = right_ref.shape[0]
    part = own_ref.shape[0]
    block = column_block(cols)
    base = lax.axis_index("narrow") * cols
    dest, begin, end = standing_numbers(numbers_ref[...], rows)
    low = picked(dest, header_ref[:, :rows].reshape(-1, width))
    left_ref[...] = low
    own_ref[...] = right_ref[pl.ds(pl.multiple_of(lax.axis_index("wide") * part, part), part), :]
    grad = jnp.zeros((2 * rows, width), F32)
    norm = jnp.zeros((8, width), F32)
    for start in range(0, cols, block):
        at = pl.ds(start, block)
        right = right_ref[at, :]
        right_low = right.astype(BF16)
        model = model_of(pair_of(low), right_low)
        real, imag, kept = residual_of(piece_ref[0, :, at], piece_ref[1, :, at], model, level_ref[:, at])
        error = masked_error(real, imag, kept, live_mask(begin, end, base + start, block))
        grad = grad + jnp.dot(error, right_low, preferred_element_type=F32)
        norm = norm + jnp.sum((right * right).reshape(-1, 8, width), 0)

    grad_ref[:rows] = grad[:rows] + unturned(grad[rows:])
    grad_ref[rows:] = jnp.broadcast_to(jnp.sum(norm, 0, keepdims=True), (PAD, width))


def step_body(mine_ref, *refs):
    *other_refs, move_ref, out_ref = refs
    total = mine_ref[...]
    for other_ref in other_refs:
        total = total + other_ref[...]
    rows = total.shape[0] - PAD
    move = (total[:rows] / (both_halves(total[rows : rows + 1]) + epsilon)).astype(BF16)
    move_ref[...] = move
    for target in range(out_ref.shape[0]):
        out_ref[target] = move


def cols_body(ways, second, header_ref, right_ref, level_ref, *refs):
    many = len(ways) or 1
    piece_refs, refs = refs[:many], refs[many:]
    if second:
        left_ref, move_ref, change_ref, out_ref, pair_ref, model_ref, error_ref, part_ref = refs
    else:
        next_ref, low_ref, left_ref, pair_ref, model_ref, error_ref = refs
    sources, tall, width = header_ref.shape
    rows = tall - PAD
    part = right_ref.shape[0]
    right = right_ref[...]
    right_low = right.astype(BF16)
    me = lax.axis_index("wide")
    base = lax.axis_index("narrow") * (sources * part) + me * part
    if level_ref.shape[1] == part:
        level = level_ref[...]
    else:
        level = level_ref[:, pl.ds(pl.multiple_of(me * part, part), part)]

    if second:
        left = left_ref[...].astype(F32) + move_ref[...].astype(F32)
        norm = jnp.sum(left * left, 0, keepdims=True)
        left_low = left.astype(BF16)
    else:
        norm = jnp.zeros((1, width), F32)
        for source in range(sources):
            norm = norm + jnp.sum(header_ref[source, rows:, :].astype(F32)[4:7], 0, keepdims=True)
        table = header_ref[:, :rows].reshape(-1, width)

    def place_pair(source, low):
        at = pl.ds(pl.multiple_of(source * 2 * rows, 2 * rows), 2 * rows)
        pair_ref[at, :] = pair_of(low)

    def pick(source):
        dest, _, _ = standing_numbers(header_ref[source, rows:, :], rows)
        low = picked(dest, table)
        left_ref[pl.ds(pl.multiple_of(source * rows, rows), rows), :] = low
        place_pair(source, low)

    def shrink(piece_real, piece_imag, source):
        at = pl.ds(pl.multiple_of(source * 2 * rows, 2 * rows), 2 * rows)
        _, begin, end = standing_numbers(header_ref[source, rows:, :], rows)
        real, imag, kept = residual_of(piece_real, piece_imag, model_ref[at, :], level)
        error_ref[at, :] = masked_error(real, imag, kept, live_mask(begin, end, base, part))

    if second:
        for source in range(sources):
            place_pair(source, left_low[source * rows : (source + 1) * rows])
    elif ways:
        for source in range(sources):
            pick(source)
    else:
        pl.loop(0, sources)(pick)

    model_ref[...] = model_of(pair_ref[...], right_low)
    for way, piece_ref in zip(ways, piece_refs):
        shrink(piece_ref[0], piece_ref[1], device_at(*way))
    if not ways:

        @pl.loop(0, sources)
        def _(source):
            shrink(piece_refs[0][source, 0], piece_refs[0][source, 1], source)

    grad = lax.dot_general(pair_ref[...], error_ref[...], (((0,), (0,)), ((), ())), preferred_element_type=F32)
    after = right + grad.T / (both_halves(norm) + epsilon)
    if not second:
        next_ref[...] = after
        low_ref[...] = after.astype(BF16)
        return
    change_ref[...] = (after - right_low.astype(F32)).astype(BF16)

    part_ref[...] = jnp.zeros_like(part_ref)

    def place_grads(source):
        at = pl.ds(pl.multiple_of(source * 2 * rows, 2 * rows), 2 * rows)
        grads = jnp.dot(error_ref[at, :], right_low, preferred_element_type=F32)
        grads = (grads[:rows] + unturned(grads[rows:])).astype(BF16)
        named = read_numbers(header_ref[source, rows:, :])[0:1, :rows].astype(jnp.int32)
        row = lax.broadcasted_iota(jnp.int32, (sources * rows, rows), 0)
        place = jnp.where(row == named, 1.0, 0.0).astype(BF16)
        part_ref[...] += jnp.dot(place, grads, preferred_element_type=F32)

    if ways:
        for source in range(sources):
            place_grads(source)
    else:
        pl.loop(0, sources)(place_grads)

    norm = jnp.sum(right * right, 0, keepdims=True)
    high = norm.astype(BF16).astype(F32)
    tail = jnp.concatenate([high, norm - high, jnp.zeros((PAD - 2, width), F32)], 0).astype(BF16)
    for target in range(sources):
        out_ref[target, :rows] = part_ref[target * rows : (target + 1) * rows].astype(BF16)
        out_ref[target, rows:] = tail


def sparse_body(ways, piece_ref, numbers_ref, left_ref, move_ref, level_ref, *refs):
    right_refs, out_ref = refs[:-1], refs[-1]
    low = (left_ref[...].astype(F32) + move_ref[...].astype(F32)).astype(BF16)
    _, begin, end = standing_numbers(numbers_ref[...], low.shape[0])
    base = lax.axis_index("narrow") * piece_ref.shape[2]

    def one(right, source):
        cols = right.shape[0]
        start = source * cols
        at = pl.ds(pl.multiple_of(start, cols), cols)
        model = model_of(pair_of(low), right)
        real, imag, kept = residual_of(piece_ref[0, :, at], piece_ref[1, :, at], model, level_ref[:, at])
        share = jnp.where(live_mask(begin, end, base + start, cols), 1.0 - kept, 0.0)
        out_ref[0, :, at] = (real * share).astype(BF16)
        out_ref[1, :, at] = (imag * share).astype(BF16)

    for way, right_ref in zip(ways, right_refs):
        one(right_ref[...], device_at(*way))
    if not ways:
        block = column_block(right_refs[0].shape[0])

        @pl.loop(0, right_refs[0].shape[0] // block)
        def _(step):
            one(right_refs[0][pl.ds(pl.multiple_of(step * block, block), block), :], step)


def join_body(ways, header_ref, move_ref, rows_ref, mine_ref, *refs):
    narrow = lax.axis_size("narrow") - 1
    other_refs, refs = refs[:narrow], refs[narrow:]
    many = len(ways) or 1
    low_refs, change_refs, refs = refs[:many], refs[many : 2 * many], refs[2 * many :]
    out_ref, rows_out_ref, held_ref, sem = refs
    copies = []
    for index, (low_ref, change_ref) in enumerate(zip(low_refs, change_refs)):
        cols = low_ref.shape[0]
        source = device_at(*ways[index]) if ways else 0
        held_ref[index] = low_ref[...].astype(F32) + change_ref[...].astype(F32)
        at = pl.ds(pl.multiple_of(source * cols, cols), cols)
        copies.append(pltpu.make_async_copy(held_ref.at[index], out_ref.at[at, :], sem.at[index]))
        copies[-1].start()

    total = mine_ref[...]
    for other_ref in other_refs:
        total = total + other_ref[...]
    rows = total.shape[0] - PAD
    norm = both_halves(total[rows : rows + 1] + total[rows + 1 : rows + 2])
    my_row = lax.axis_index("wide") * rows + lax.broadcasted_iota(jnp.int32, (rows, rows), 0)
    first = jnp.zeros(rows_ref.shape, F32)
    for source in range(header_ref.shape[0]):
        named = read_numbers(header_ref[source, rows:, :])[0:1, :rows].astype(jnp.int32)
        place = jnp.where(my_row == named, 1.0, 0.0).astype(BF16)
        first = first + jnp.dot(place, move_ref[source], preferred_element_type=F32)
    rows_out_ref[...] = rows_ref[...] + first + total[:rows] / (norm + epsilon)
    for copy in copies:
        copy.wait()


VMEM = pl.BlockSpec(memory_space=pltpu.VMEM)


SMALL = 400000


def small(value):
    return math.prod(value.shape) * jnp.dtype(value.dtype).itemsize < SMALL


ANY = pl.BlockSpec(memory_space=pl.ANY)


def call(body, name, shapes, arrays, scratch=(), out_specs=None, keep=True):
    if keep:
        shapes = jax.tree.map(lambda v: pltpu.VMEM(v.shape, v.dtype) if small(v) else v, shapes)
    if name != "prep":
        arrays = [pltpu.with_memory_space_constraint(v, pltpu.VMEM) if small(v) else v for v in arrays]
    return pl.pallas_call(
        body,
        in_specs=[VMEM] * len(arrays),
        out_specs=out_specs or jax.tree.map(lambda _: VMEM, shapes),
        out_shape=shapes,
        scratch_shapes=list(scratch),
    )(*arrays)


def column_block(count):
    block = min(512, count)
    while count % block:
        block //= 2
    return block


def exchange(blocks):
    return lax.all_to_all(blocks, "wide", split_axis=0, concat_axis=0, tiled=True)


def other_narrow(value):
    count = lax.axis_size("narrow")
    return [lax.ppermute(value, "narrow", [(i, (i + k) % count) for i in range(count)]) for k in range(1, count)]


def small_wide():
    return lax.axis_size("wide") in (NEAR, 2 * NEAR, 4 * NEAR)


def shift(value, far, near):
    outer = lax.axis_size("wide") // NEAR
    pairs = [
        (z * NEAR + x, (z ^ far) * NEAR + (x ^ near)) for z in range(outer) for x in range(NEAR)
    ]
    return lax.ppermute(value, "wide", pairs)


def device_at(far, near):
    me = lax.axis_index("wide")
    return ((me // NEAR) ^ far) * NEAR + ((me % NEAR) ^ near)


PART_ORDER = ((3, 0), (3, 1), (0, 1), (1, 1), (1, 0), (2, 1), (2, 0), (0, 0))


def part_ways():
    if not small_wide():
        return ()
    return tuple(way for way in PART_ORDER if way[0] < lax.axis_size("wide") // NEAR)


def gather_ways():
    if not small_wide():
        return ()
    return tuple((far, near) for far in range(lax.axis_size("wide") // NEAR) for near in range(NEAR))


def gather_parts(block):
    count = lax.axis_size("wide")
    ways = gather_ways()
    if not ways:
        return [exchange(jnp.broadcast_to(block[None], (count,) + block.shape)).reshape(-1, block.shape[1])]
    outer = count // NEAR
    held = {(0, 0): block}
    far = 1
    while far < outer:
        held[far, 0] = shift(block, far, 0)
        far *= 2
    held[0, 1] = shift(block, 0, 1)
    for way in reversed(ways):
        if way not in held and way[0] < 3 and way[1]:
            held[way] = shift(held[way[0], 0], 0, way[1])
    if outer == 4 and (3, 0) not in held:
        held[3, 0] = shift(held[2, 0], 1, 0)
    for way in ways:
        if way not in held:
            held[way] = shift(held[2, 1], 1, 0)
    return [held[way] for way in ways]


def program(pieces, destination, first_offset, valid_length, midpoint_factor, offset_factor, threshold):
    count = lax.axis_size("wide")
    _, rows, cols = pieces.shape
    width = offset_factor.shape[1]
    part = cols // count
    total = count * rows
    level = threshold[None, :]

    ways = part_ways()
    shape = jax.ShapeDtypeStruct
    header, numbers, level, *parts = call(
        partial(prep_body, ways),
        "prep",
        [shape((count, rows + PAD, width), BF16), pltpu.VMEM((PAD, width), BF16), pltpu.VMEM(level.shape, F32)]
        + [shape((2, rows, part), pieces.dtype)] * len(ways),
        [midpoint_factor, destination[None], first_offset[None], valid_length[None], level] + [pieces] * bool(ways),
        keep=False,
    )
    own_level = level
    if part % 128:
        own_level = lax.dynamic_slice_in_dim(level, lax.axis_index("wide") * part, part, 1)
    headers = exchange(header)
    if ways:
        blocks = []
        for way, block in zip(ways, parts):
            blocks.append(block if way == (0, 0) else shift(block, *way))
    else:
        blocks = [exchange(jnp.transpose(pieces.reshape(2, rows, count, part), (2, 0, 1, 3)))]

    row_grad, left_mine, own_right = call(
        rows_body,
        "row_pass",
        [shape((rows + PAD, width), F32), shape((rows, width), BF16), shape((part, width), F32)],
        [pieces, headers, numbers, offset_factor, level],
    )
    move_mine, moves = call(
        step_body,
        "step",
        [shape((rows, width), BF16), shape((count, rows, width), BF16)],
        [row_grad] + other_narrow(row_grad),
    )
    moves = exchange(moves)

    held = [pltpu.VMEM((2 * total, width), BF16), pltpu.VMEM((2 * total, part), F32), pltpu.VMEM((2 * total, part), BF16)]
    right_one, right_low, left_all = call(
        partial(cols_body, ways, False),
        "col_pass_1",
        [shape((part, width), F32), shape((part, width), BF16), shape((total, width), BF16)],
        [headers, own_right, own_level, *blocks],
        held,
    )
    lows = gather_parts(right_low)

    change, outgoing = call(
        partial(cols_body, ways, True),
        "col_pass_2",
        [shape((part, width), BF16), shape((count, rows + PAD, width), BF16)],
        [headers, right_one, own_level, *blocks, left_all, moves.reshape(total, width)],
        [*held, pltpu.VMEM((total, width), F32)],
    )
    changes = gather_parts(change)
    arrived = exchange(outgoing)
    summed = jnp.sum(arrived.astype(F32), 0)

    sparse = call(
        partial(sparse_body, gather_ways()),
        "sparse_pass",
        shape(pieces.shape, BF16),
        [pieces, numbers, left_mine, move_mine, level, *lows],
        keep=False,
    )
    new_offset, new_midpoint = call(
        partial(join_body, gather_ways()),
        "join",
        [shape((cols, width), F32), shape((rows, width), F32)],
        [headers, moves, midpoint_factor, summed, *other_narrow(summed), *lows, *changes],
        [pltpu.VMEM((len(lows), cols // len(lows), width), F32), pltpu.SemaphoreType.DMA((len(lows),))],
        [ANY, VMEM],
        keep=False,
    )
    return sparse, new_midpoint, new_offset


def solution(mesh):
    placed = (
        P(None, ("groups", "wide"), "narrow"),
        P("wide"),
        P("wide"),
        P("wide"),
        P(("groups", "wide"), None),
        P(("groups", "narrow"), None),
        P(("groups", "narrow")),
    )
    return jax.shard_map(
        program,
        mesh=mesh,
        in_specs=placed,
        out_specs=(
            P(None, ("groups", "wide"), "narrow"),
            P(("groups", "wide"), None),
            P(("groups", "narrow"), None),
        ),
        check_vma=False,
    )
```

```python
import math
from functools import partial

import jax
import jax.numpy as jnp
from jax import lax
from jax.experimental import pallas as pl
from jax.experimental.pallas import tpu as pltpu
from jax.sharding import PartitionSpec as P


epsilon = 1e-06
F32 = jnp.float32
BF16 = jnp.bfloat16
PAD = 8
NEAR = 2


def turned(rows):
    half = rows.shape[1] // 2
    return jnp.concatenate([rows[:, half:], -rows[:, :half]], 1)


def unturned(rows):
    half = rows.shape[1] // 2
    return jnp.concatenate([-rows[:, half:], rows[:, :half]], 1)


def both_halves(norm):
    half = norm.shape[1] // 2
    once = norm[:, :half] + norm[:, half:]
    return jnp.concatenate([once, once], 1)


def pair_of(left_low):
    return jnp.concatenate([left_low, turned(left_low)], 0)


def model_of(pair, right_low):
    return lax.dot_general(pair, right_low, (((1,), (1,)), ((), ())), preferred_element_type=F32)


def residual_of(piece_real, piece_imag, model, level):
    rows = model.shape[0] // 2
    real = piece_real.astype(F32) - model[:rows]
    imag = piece_imag.astype(F32) - model[rows:]
    kept = level * lax.rsqrt(jnp.maximum(real * real + imag * imag, level * level))
    return real, imag, kept


def live_mask(begin, end, first_col, count):
    column = lax.broadcasted_iota(jnp.int32, (begin.shape[0], count), 1)
    return (column >= begin - first_col) & (column < end - first_col)


def masked_error(real, imag, kept, inside):
    share = jnp.where(inside, kept, 0.0)
    return jnp.concatenate([(real * share).astype(BF16), (imag * share).astype(BF16)], 0)


BASE = 128


def row_numbers(dest_ref, first_ref, valid_ref, rows_ref):
    first = first_ref[...]
    end = first + valid_ref[...]
    both = jnp.concatenate(
        [jnp.concatenate([dest_ref[...], first], 1), jnp.concatenate([end, jnp.zeros_like(end)], 1)], 0
    )
    high = both >> (BASE.bit_length() - 1)
    table = rows_ref[...]
    norm = [way.astype(F32) for way in three_ways(jnp.sum(table * table, 0, keepdims=True))]
    low = (both & (BASE - 1)).astype(F32)
    return jnp.concatenate([high.astype(F32), low, *norm, jnp.zeros((PAD - 7, table.shape[1]), F32)], 0).astype(BF16)


def read_numbers(numbers):
    value = numbers.astype(F32)
    return value[0:2] * BASE + value[2:4]


def standing_numbers(numbers, rows):
    value = read_numbers(numbers)
    value = jnp.concatenate([value, jnp.zeros((6, value.shape[1]), F32)], 0)
    columns = value.T.astype(jnp.int32)
    return columns[:rows, 0:1], columns[rows : 2 * rows, 0:1], columns[:rows, 1:2]


def three_ways(table):
    high = table.astype(BF16)
    rest = table - high.astype(F32)
    middle = rest.astype(BF16)
    return [high, middle, (rest - middle.astype(F32)).astype(BF16)]


def picked(dest, table):
    row = lax.broadcasted_iota(jnp.int32, (dest.shape[0], table.shape[0]), 1)
    place = jnp.where(row == dest, 1.0, 0.0).astype(BF16)
    return jnp.dot(place, table, preferred_element_type=F32).astype(BF16)


def prep_body(ways, rows_ref, dest_ref, first_ref, valid_ref, *refs):
    level_in_ref, *refs = refs
    piece_ref, header_ref, numbers_ref, level_ref, *part_refs = refs if ways else (None, *refs)
    level_ref[...] = level_in_ref[...]
    count, tall, _ = header_ref.shape
    rows = tall - PAD
    numbers = row_numbers(dest_ref, first_ref, valid_ref, rows_ref)
    numbers_ref[...] = numbers
    low = rows_ref[...].astype(BF16)
    for target in range(count):
        header_ref[target, :rows] = low
        header_ref[target, rows:] = numbers
    for way, part_ref in zip(ways, part_refs):
        cols = part_ref.shape[2]
        part_ref[...] = piece_ref[:, :, pl.ds(pl.multiple_of(device_at(*way) * cols, cols), cols)]


def rows_body(piece_ref, header_ref, numbers_ref, right_ref, level_ref, *refs):
    grad_ref, left_ref, own_ref = refs
    rows, width = left_ref.shape
    cols = right_ref.shape[0]
    part = own_ref.shape[0]
    block = column_block(cols)
    base = lax.axis_index("narrow") * cols
    dest, begin, end = standing_numbers(numbers_ref[...], rows)
    low = picked(dest, header_ref[:, :rows].reshape(-1, width))
    left_ref[...] = low
    own_ref[...] = right_ref[pl.ds(pl.multiple_of(lax.axis_index("wide") * part, part), part), :]
    grad = jnp.zeros((2 * rows, width), F32)
    norm = jnp.zeros((8, width), F32)
    for start in range(0, cols, block):
        at = pl.ds(start, block)
        right = right_ref[at, :]
        right_low = right.astype(BF16)
        model = model_of(pair_of(low), right_low)
        real, imag, kept = residual_of(piece_ref[0, :, at], piece_ref[1, :, at], model, level_ref[:, at])
        error = masked_error(real, imag, kept, live_mask(begin, end, base + start, block))
        grad = grad + jnp.dot(error, right_low, preferred_element_type=F32)
        norm = norm + jnp.sum((right * right).reshape(-1, 8, width), 0)

    grad_ref[:rows] = grad[:rows] + unturned(grad[rows:])
    grad_ref[rows:] = jnp.broadcast_to(jnp.sum(norm, 0, keepdims=True), (PAD, width))


def step_body(mine_ref, *refs):
    *other_refs, move_ref, out_ref = refs
    total = mine_ref[...]
    for other_ref in other_refs:
        total = total + other_ref[...]
    rows = total.shape[0] - PAD
    move = (total[:rows] / (both_halves(total[rows : rows + 1]) + epsilon)).astype(BF16)
    move_ref[...] = move
    for target in range(out_ref.shape[0]):
        out_ref[target] = move


def cols_body(ways, second, header_ref, right_ref, level_ref, *refs):
    many = len(ways) or 1
    piece_refs, refs = refs[:many], refs[many:]
    if second:
        left_ref, move_ref, change_ref, out_ref, pair_ref, model_ref, error_ref, part_ref = refs
    else:
        next_ref, low_ref, left_ref, pair_ref, model_ref, error_ref = refs
    sources, tall, width = header_ref.shape
    rows = tall - PAD
    part = right_ref.shape[0]
    right = right_ref[...]
    right_low = right.astype(BF16)
    me = lax.axis_index("wide")
    base = lax.axis_index("narrow") * (sources * part) + me * part
    if level_ref.shape[1] == part:
        level = level_ref[...]
    else:
        level = level_ref[:, pl.ds(pl.multiple_of(me * part, part), part)]

    if second:
        left = left_ref[...].astype(F32) + move_ref[...].astype(F32)
        norm = jnp.sum(left * left, 0, keepdims=True)
        left_low = left.astype(BF16)
    else:
        norm = jnp.zeros((1, width), F32)
        for source in range(sources):
            norm = norm + jnp.sum(header_ref[source, rows:, :].astype(F32)[4:7], 0, keepdims=True)
        table = header_ref[:, :rows].reshape(-1, width)

    def place_pair(source, low):
        at = pl.ds(pl.multiple_of(source * 2 * rows, 2 * rows), 2 * rows)
        pair_ref[at, :] = pair_of(low)

    def pick(source):
        dest, _, _ = standing_numbers(header_ref[source, rows:, :], rows)
        low = picked(dest, table)
        left_ref[pl.ds(pl.multiple_of(source * rows, rows), rows), :] = low
        place_pair(source, low)

    def shrink(piece_real, piece_imag, source):
        at = pl.ds(pl.multiple_of(source * 2 * rows, 2 * rows), 2 * rows)
        _, begin, end = standing_numbers(header_ref[source, rows:, :], rows)
        real, imag, kept = residual_of(piece_real, piece_imag, model_ref[at, :], level)
        error_ref[at, :] = masked_error(real, imag, kept, live_mask(begin, end, base, part))

    if second:
        for source in range(sources):
            place_pair(source, left_low[source * rows : (source + 1) * rows])
    elif ways:
        for source in range(sources):
            pick(source)
    else:
        pl.loop(0, sources)(pick)

    model_ref[...] = model_of(pair_ref[...], right_low)
    for way, piece_ref in zip(ways, piece_refs):
        shrink(piece_ref[0], piece_ref[1], device_at(*way))
    if not ways:

        @pl.loop(0, sources)
        def _(source):
            shrink(piece_refs[0][source, 0], piece_refs[0][source, 1], source)

    grad = lax.dot_general(pair_ref[...], error_ref[...], (((0,), (0,)), ((), ())), preferred_element_type=F32)
    after = right + grad.T / (both_halves(norm) + epsilon)
    if not second:
        next_ref[...] = after
        low_ref[...] = after.astype(BF16)
        return
    change_ref[...] = (after - right_low.astype(F32)).astype(BF16)

    part_ref[...] = jnp.zeros_like(part_ref)

    def place_grads(source):
        at = pl.ds(pl.multiple_of(source * 2 * rows, 2 * rows), 2 * rows)
        grads = jnp.dot(error_ref[at, :], right_low, preferred_element_type=F32)
        grads = (grads[:rows] + unturned(grads[rows:])).astype(BF16)
        named = read_numbers(header_ref[source, rows:, :])[0:1, :rows].astype(jnp.int32)
        row = lax.broadcasted_iota(jnp.int32, (sources * rows, rows), 0)
        place = jnp.where(row == named, 1.0, 0.0).astype(BF16)
        part_ref[...] += jnp.dot(place, grads, preferred_element_type=F32)

    if ways:
        for source in range(sources):
            place_grads(source)
    else:
        pl.loop(0, sources)(place_grads)

    norm = jnp.sum(right * right, 0, keepdims=True)
    high = norm.astype(BF16).astype(F32)
    tail = jnp.concatenate([high, norm - high, jnp.zeros((PAD - 2, width), F32)], 0).astype(BF16)
    for target in range(sources):
        out_ref[target, :rows] = part_ref[target * rows : (target + 1) * rows].astype(BF16)
        out_ref[target, rows:] = tail


def sparse_body(ways, piece_ref, numbers_ref, left_ref, move_ref, level_ref, *refs):
    *right_refs, out_hbm, out_ref, sem = refs
    copies = []
    low = (left_ref[...].astype(F32) + move_ref[...].astype(F32)).astype(BF16)
    _, begin, end = standing_numbers(numbers_ref[...], low.shape[0])
    base = lax.axis_index("narrow") * piece_ref.shape[2]

    def one(right, source):
        cols = right.shape[0]
        start = source * cols
        at = pl.ds(pl.multiple_of(start, cols), cols)
        model = model_of(pair_of(low), right)
        real, imag, kept = residual_of(piece_ref[0, :, at], piece_ref[1, :, at], model, level_ref[:, at])
        share = jnp.where(live_mask(begin, end, base + start, cols), 1.0 - kept, 0.0)
        out_ref[0, :, at] = (real * share).astype(BF16)
        out_ref[1, :, at] = (imag * share).astype(BF16)

    for index, (way, right_ref) in enumerate(zip(ways, right_refs)):
        one(right_ref[...], device_at(*way))
        part = right_ref.shape[0]
        at = pl.ds(pl.multiple_of(device_at(*way) * part, part), part)
        copies.append(pltpu.make_async_copy(out_ref.at[:, :, at], out_hbm.at[:, :, at], sem.at[index]))
        copies[-1].start()
    if not ways:
        block = column_block(right_refs[0].shape[0])

        @pl.loop(0, right_refs[0].shape[0] // block)
        def _(step):
            one(right_refs[0][pl.ds(pl.multiple_of(step * block, block), block), :], step)

        copies.append(pltpu.make_async_copy(out_ref, out_hbm, sem.at[0]))
        copies[-1].start()
    for copy in copies:
        copy.wait()


def join_body(ways, header_ref, move_ref, rows_ref, mine_ref, *refs):
    narrow = lax.axis_size("narrow") - 1
    other_refs, refs = refs[:narrow], refs[narrow:]
    many = len(ways) or 1
    low_refs, change_refs, refs = refs[:many], refs[many : 2 * many], refs[2 * many :]
    out_ref, rows_out_ref, held_ref, sem = refs
    copies = []
    for index, (low_ref, change_ref) in enumerate(zip(low_refs, change_refs)):
        cols = low_ref.shape[0]
        source = device_at(*ways[index]) if ways else 0
        held_ref[index] = low_ref[...].astype(F32) + change_ref[...].astype(F32)
        at = pl.ds(pl.multiple_of(source * cols, cols), cols)
        copies.append(pltpu.make_async_copy(held_ref.at[index], out_ref.at[at, :], sem.at[index]))
        copies[-1].start()

    total = mine_ref[...]
    for other_ref in other_refs:
        total = total + other_ref[...]
    rows = total.shape[0] - PAD
    norm = both_halves(total[rows : rows + 1] + total[rows + 1 : rows + 2])
    my_row = lax.axis_index("wide") * rows + lax.broadcasted_iota(jnp.int32, (rows, rows), 0)
    first = jnp.zeros(rows_ref.shape, F32)
    for source in range(header_ref.shape[0]):
        named = read_numbers(header_ref[source, rows:, :])[0:1, :rows].astype(jnp.int32)
        place = jnp.where(my_row == named, 1.0, 0.0).astype(BF16)
        first = first + jnp.dot(place, move_ref[source], preferred_element_type=F32)
    rows_out_ref[...] = rows_ref[...] + first + total[:rows] / (norm + epsilon)
    for copy in copies:
        copy.wait()


VMEM = pl.BlockSpec(memory_space=pltpu.VMEM)


SMALL = 400000


def small(value):
    return math.prod(value.shape) * jnp.dtype(value.dtype).itemsize < SMALL


ANY = pl.BlockSpec(memory_space=pl.ANY)


def call(body, name, shapes, arrays, scratch=(), out_specs=None, keep=True):
    if keep:
        shapes = jax.tree.map(lambda v: pltpu.VMEM(v.shape, v.dtype) if small(v) else v, shapes)
    if name != "prep":
        arrays = [pltpu.with_memory_space_constraint(v, pltpu.VMEM) if small(v) else v for v in arrays]
    return pl.pallas_call(
        body,
        in_specs=[VMEM] * len(arrays),
        out_specs=out_specs or jax.tree.map(lambda _: VMEM, shapes),
        out_shape=shapes,
        scratch_shapes=list(scratch),
    )(*arrays)


def column_block(count):
    block = min(512, count)
    while count % block:
        block //= 2
    return block


def exchange(blocks):
    return lax.all_to_all(blocks, "wide", split_axis=0, concat_axis=0, tiled=True)


def other_narrow(value):
    count = lax.axis_size("narrow")
    return [lax.ppermute(value, "narrow", [(i, (i + k) % count) for i in range(count)]) for k in range(1, count)]


def small_wide():
    return lax.axis_size("wide") in (NEAR, 2 * NEAR, 4 * NEAR)


def shift(value, far, near):
    outer = lax.axis_size("wide") // NEAR
    pairs = [
        (z * NEAR + x, (z ^ far) * NEAR + (x ^ near)) for z in range(outer) for x in range(NEAR)
    ]
    return lax.ppermute(value, "wide", pairs)


def device_at(far, near):
    me = lax.axis_index("wide")
    return ((me // NEAR) ^ far) * NEAR + ((me % NEAR) ^ near)


PART_ORDER = ((3, 0), (3, 1), (1, 1), (1, 0), (0, 1), (2, 1), (2, 0), (0, 0))


def part_ways():
    if not small_wide():
        return ()
    return tuple(way for way in PART_ORDER if way[0] < lax.axis_size("wide") // NEAR)


def gather_ways():
    if not small_wide():
        return ()
    return tuple((far, near) for far in range(lax.axis_size("wide") // NEAR) for near in range(NEAR))


def gather_parts(block):
    count = lax.axis_size("wide")
    ways = gather_ways()
    if not ways:
        return [exchange(jnp.broadcast_to(block[None], (count,) + block.shape)).reshape(-1, block.shape[1])]
    outer = count // NEAR
    held = {(0, 0): block}
    far = 1
    while far < outer:
        held[far, 0] = shift(block, far, 0)
        far *= 2
    held[0, 1] = shift(block, 0, 1)
    for way in reversed(ways):
        if way not in held and way[0] < 3 and way[1]:
            held[way] = shift(held[way[0], 0], 0, way[1])
    if outer == 4 and (3, 0) not in held:
        held[3, 0] = shift(held[2, 0], 1, 0)
    for way in ways:
        if way not in held:
            held[way] = shift(held[2, 1], 1, 0)
    return [held[way] for way in ways]


def program(pieces, destination, first_offset, valid_length, midpoint_factor, offset_factor, threshold):
    count = lax.axis_size("wide")
    _, rows, cols = pieces.shape
    width = offset_factor.shape[1]
    part = cols // count
    total = count * rows
    level = threshold[None, :]

    ways = part_ways()
    shape = jax.ShapeDtypeStruct
    header, numbers, level, *parts = call(
        partial(prep_body, ways),
        "prep",
        [shape((count, rows + PAD, width), BF16), pltpu.VMEM((PAD, width), BF16), pltpu.VMEM(level.shape, F32)]
        + [
            pltpu.VMEM((2, rows, part), pieces.dtype) if way == (0, 0) else shape((2, rows, part), pieces.dtype)
            for way in ways
        ],
        [midpoint_factor, destination[None], first_offset[None], valid_length[None], level] + [pieces] * bool(ways),
        keep=False,
    )
    own_level = level
    if part % 128:
        own_level = lax.dynamic_slice_in_dim(level, lax.axis_index("wide") * part, part, 1)
    headers = exchange(header)
    if ways:
        blocks = []
        for way, block in zip(ways, parts):
            blocks.append(block if way == (0, 0) else shift(block, *way))
    else:
        blocks = [exchange(jnp.transpose(pieces.reshape(2, rows, count, part), (2, 0, 1, 3)))]

    row_grad, left_mine, own_right = call(
        rows_body,
        "row_pass",
        [shape((rows + PAD, width), F32), shape((rows, width), BF16), shape((part, width), F32)],
        [pieces, headers, numbers, offset_factor, level],
    )
    move_mine, moves = call(
        step_body,
        "step",
        [shape((rows, width), BF16), shape((count, rows, width), BF16)],
        [row_grad] + other_narrow(row_grad),
    )
    moves = exchange(moves)

    held = [pltpu.VMEM((2 * total, width), BF16), pltpu.VMEM((2 * total, part), F32), pltpu.VMEM((2 * total, part), BF16)]
    right_one, right_low, left_all = call(
        partial(cols_body, ways, False),
        "col_pass_1",
        [shape((part, width), F32), shape((part, width), BF16), shape((total, width), BF16)],
        [headers, own_right, own_level, *blocks],
        held,
    )
    lows = gather_parts(right_low)

    change, outgoing = call(
        partial(cols_body, ways, True),
        "col_pass_2",
        [shape((part, width), BF16), shape((count, rows + PAD, width), BF16)],
        [headers, right_one, own_level, *blocks, left_all, moves.reshape(total, width)],
        [*held, pltpu.VMEM((total, width), F32)],
    )
    changes = gather_parts(change)
    arrived = exchange(outgoing)
    summed = jnp.sum(arrived.astype(F32), 0)

    sparse = call(
        partial(sparse_body, gather_ways()),
        "sparse_pass",
        shape(pieces.shape, BF16),
        [pieces, numbers, left_mine, move_mine, level, *lows],
        [pltpu.VMEM(pieces.shape, BF16), pltpu.SemaphoreType.DMA((len(lows),))],
        ANY,
        keep=False,
    )
    new_offset, new_midpoint = call(
        partial(join_body, gather_ways()),
        "join",
        [shape((cols, width), F32), shape((rows, width), F32)],
        [headers, moves, midpoint_factor, summed, *other_narrow(summed), *lows, *changes],
        [pltpu.VMEM((len(lows), cols // len(lows), width), F32), pltpu.SemaphoreType.DMA((len(lows),))],
        [ANY, VMEM],
        keep=False,
    )
    return sparse, new_midpoint, new_offset


def solution(mesh):
    placed = (
        P(None, ("groups", "wide"), "narrow"),
        P("wide"),
        P("wide"),
        P("wide"),
        P(("groups", "wide"), None),
        P(("groups", "narrow"), None),
        P(("groups", "narrow")),
    )
    return jax.shard_map(
        program,
        mesh=mesh,
        in_specs=placed,
        out_specs=(
            P(None, ("groups", "wide"), "narrow"),
            P(("groups", "wide"), None),
            P(("groups", "narrow"), None),
        ),
        check_vma=False,
    )
```
